256 devices in a mesh: row: 16 (over z, y_lo), col: 16 (over y_hi, x, core).
Axes of the slice: x: 4, y: 4 (y_hi: 2, y_lo: 2; y = y_hi * 2 + y_lo), z: 8, core: 2. Of those that a mesh axis runs over, the one named last changes fastest.
Arguments:
- adjoint_source: float32 [192, 256, 2, 128], P('row', 'col'), may hold values from -6 to 6
- saved_currents: float32 [192, 256, 2, 128], P('row', 'col'), may hold values from -6 to 6
- lag_blocks: float32 [7, 7, 2, 128, 128], replicated, may hold values from -0.01875 to 0.01875
- element_inverse: float32 [2, 128, 128], replicated, may hold values from -0.088388348 to 1.0883883
Outputs:
- adjoint: float32 [192, 256, 2, 128], P('row', 'col')
- lag_grad: float32 [7, 7, 2, 128, 128], P(None, None, None, 'row')
The draws below stay inside these ranges and needn't reach their ends.
All inputs are finite; a program needn't handle non-finite values.
Results may differ from the reference program's by a relative error of at most 0.0001.
Values sent between devices are 32-bit elements; how exact they have to be, the bound alone decides.
A program may use at most 128 MiB of HBM per device.

```python
import math
import jax
import jax.numpy as jnp
from jax import lax

M = 128
REACH = 3
SPAN = 7
SWEEPS = 2
NR = 192
NC = 256


def draw_element_inverse(key, part):
    noise_key = jax.random.fold_in(key, 17)
    noise = jnp.clip(jax.random.normal(noise_key, (2, M, M), jnp.float32), -5.0, 5.0)
    noise = noise * (0.2 / math.sqrt(M))
    identity = jnp.eye(M, dtype=jnp.float32)
    return noise + jnp.stack((identity, jnp.zeros_like(identity)))


def steps_of(own_key, extent, split, smallest, high):
    def one(axis_at, parts):
        draws = jax.random.uniform(jax.random.fold_in(jax.random.fold_in(own_key, 6), axis_at), (parts,), jnp.float32, smallest / len(split), high / len(split))
        return jnp.repeat(jnp.exp(draws), extent[axis_at] // parts).reshape((-1,) + (1,) * (len(extent) - axis_at - 1))

    gain = one(*split[0])
    for cut in split[1:]:
        gain = gain * one(*cut)
    return gain


def gaussian(rng, shape, width, most, split=(), kind=jnp.bfloat16):
    entries = width * jax.random.normal(rng, shape, jnp.float32)
    if split:
        entries = entries * steps_of(rng, shape, split, -0.22, 0.18)
    return jnp.clip(entries, -most, most).astype(kind)


def setup_inputs(seed: int = 0) -> dict:
    arg_keys = jax.random.split(jax.random.key(seed), 5)
    adjoint_source = gaussian(arg_keys[0], (NR, NC, 2, M), 1.0, 6.0, ((0, 16), (1, 16)), jnp.float32)
    saved_currents = gaussian(arg_keys[1], (NR, NC, 2, M), 1.0, 6.0, ((0, 16), (1, 16)), jnp.float32)
    lag_blocks = gaussian(arg_keys[2], (SPAN, SPAN, 2, M, M), (0.35 * (98 * M) ** -0.5), 0.01875, (), jnp.float32)
    element_inverse = draw_element_inverse(jax.random.fold_in(arg_keys[4], 71), 0)
    return {"adjoint_source": adjoint_source, "saved_currents": saved_currents, "lag_blocks": lag_blocks, "element_inverse": element_inverse}


precise = lax.Precision.HIGHEST

def combine_parts(product):
    real = product[..., 0, 0, :] + product[..., 1, 1, :]
    imag = product[..., 1, 0, :] - product[..., 0, 1, :]
    return jnp.stack((real, imag), axis=-2)

def conj_apply(field, blocks):
    product = jnp.einsum('ijkm,cmq->ijkcq', field, blocks, precision=precise)
    return combine_parts(product)

def lag_apply(padded, lag_blocks, rows, cols):
    span = lag_blocks.shape[0]
    accum = None
    for offset_row in range(span):
        stacked = jnp.stack([padded[offset_row:offset_row + rows, offset_col:offset_col + cols] for offset_col in range(span)])
        product = jnp.einsum('bijkm,bcmq->ijkcq', stacked, lag_blocks[offset_row], precision=precise)
        accum = product if accum is None else accum + product
    return combine_parts(accum)

def correlate(adjoint, current_pad, span, rows, cols):
    layers = []
    for offset_row in range(span):
        first = span - 1 - offset_row
        stacked = jnp.stack([current_pad[first:first + rows, span - 1 - offset_col:span - 1 - offset_col + cols] for offset_col in range(span)])
        product = jnp.einsum('ijkm,bijhq->bkmhq', adjoint, stacked, precision=precise)
        real = product[:, 0, :, 0] + product[:, 1, :, 1]
        imag = product[:, 1, :, 0] - product[:, 0, :, 1]
        layers.append(jnp.stack((real, imag), axis=1))
    return jnp.stack(layers)

def reference(adjoint_source, saved_currents, lag_blocks, element_inverse):
    widths = ((REACH, REACH), (REACH, REACH), (0, 0), (0, 0))
    adjoint = conj_apply(adjoint_source, element_inverse)
    for sweep in range(SWEEPS):
        padded = jnp.pad(adjoint, widths)
        image = adjoint + lag_apply(padded, lag_blocks, NR, NC)
        adjoint = adjoint + conj_apply(adjoint_source - image, element_inverse)
    current_pad = jnp.pad(saved_currents, widths)
    factor = -1.0 / math.sqrt(NR * NC)
    lag_grad = correlate(adjoint, current_pad, SPAN, NR, NC) * factor
    return (adjoint, lag_grad)
```

```python
import functools
import math

import jax
import jax.numpy as jnp
from jax import lax
from jax.experimental import pallas as pl
from jax.experimental.pallas import tpu as pltpu
from jax.sharding import PartitionSpec as P

SWEEPS = 2
F32 = jnp.float32
BF16 = jnp.bfloat16
MESH = pl.DeviceIdType.MESH
DIRS = tuple((dr, dc) for dr in (-1, 0, 1) for dc in (-1, 0, 1) if (dr, dc) != (0, 0))


def split(x):
    hi = x.astype(BF16)
    lo = (x - hi.astype(F32)).astype(BF16)
    return hi, lo


def dot(x, y):
    return jnp.dot(x, y, preferred_element_type=F32)


def put_embedded(dst, base, a0, a1):
    dst[pl.ds(base, 128), 0:128] = a0
    dst[pl.ds(base, 128), 128:256] = -a1
    dst[pl.ds(base + 128, 128), 0:128] = a1
    dst[pl.ds(base + 128, 128), 128:256] = a0


def field(ref, rows, start, cols):
    re = ref[rows, pl.ds(start, cols, stride=2), :]
    im = ref[rows, pl.ds(start + 1, cols, stride=2), :]
    return re, im


def sweeps_kernel(
    src, lag, inv, out,
    stage, whi, wlo, vhi, vlo, ext, shifted, acc, adj,
    lag_sem, send_sem, recv_sem,
):
    peers_r, peers_c = lax.axis_size("row"), lax.axis_size("col")
    r, c = lax.axis_index("row"), lax.axis_index("col")

    def lag_copy(a):
        return pltpu.make_async_copy(lag.at[a], stage.at[a], lag_sem.at[a])

    for a in range(7):
        lag_copy(a).start()

    def at(dr, dc):
        return (lax.rem(r + dr + peers_r, peers_r), lax.rem(c + dc + peers_c, peers_c))

    barrier = pltpu.get_barrier_semaphore()
    for dr, dc in DIRS:
        pl.semaphore_signal(barrier, inc=1, device_id=at(dr, dc), device_id_type=MESH)

    def box(dr, dc):
        rows = {-1: (3, 15, 3), 1: (12, 0, 3), 0: (3, 3, 12)}[dr]
        cols = {-1: (8, 40, 8), 1: (32, 0, 8), 0: (8, 8, 32)}[dc]
        return rows, cols

    def halo_copy(s, d):
        dr, dc = DIRS[d]
        (rs, rd, rn), (cs, cd, cn) = box(dr, dc)
        return pltpu.make_async_remote_copy(
            src_ref=ext.at[s, pl.ds(rs, rn), pl.ds(cs, cn), :],
            dst_ref=ext.at[s, pl.ds(rd, rn), pl.ds(cd, cn), :],
            send_sem=send_sem.at[s, d],
            recv_sem=recv_sem.at[s, d],
            device_id=at(dr, dc),
            device_id_type=MESH,
        )

    b0h, b0l = split(inv[0])
    b1h, b1l = split(inv[1])
    put_embedded(vhi, 0, b0h, b1h)
    put_embedded(vlo, 0, b0l, b1l)

    def apply_inverse(x):
        xh, xl = split(x)
        return dot(xh, vhi[...]) + dot(xl, vhi[...]) + dot(xh, vlo[...])

    def source():
        re, im = field(src, slice(None), 0, 16)
        return jnp.concatenate([re.reshape(192, 128), im.reshape(192, 128)], axis=1)

    def publish(ref, at_, x):
        rows, start = at_
        ref[rows, pl.ds(start, 16, stride=2), :] = x[:, :128].reshape(12, 16, 128)
        ref[rows, pl.ds(start + 1, 16, stride=2), :] = x[:, 128:].reshape(12, 16, 128)

    adj[...] = apply_inverse(source())
    publish(ext.at[0], (slice(3, 15), 8), adj[...])
    pl.semaphore_wait(barrier, len(DIRS))

    for s in range(SWEEPS):
        for d in range(len(DIRS)):
            halo_copy(s, d).start()
        if s == 0:
            def prepare(a, carry):
                lag_copy(a).wait()

                def one(b, carry):
                    h0, l0 = split(stage[a, b, 0])
                    h1, l1 = split(stage[a, b, 1])
                    base = pl.multiple_of(b * 256, 256)
                    put_embedded(whi.at[a], base, h0, h1)
                    put_embedded(wlo.at[a], base, l0, l1)
                    return carry

                return lax.fori_loop(0, 7, one, carry)

            lax.fori_loop(0, 7, prepare, 0)
        for d in range(len(DIRS)):
            halo_copy(s, d).wait_send()
        for d in range(len(DIRS)):
            halo_copy(s, d).wait_recv()

        @pl.when(r == 0)
        def _():
            ext[s, 0:3] = jnp.zeros((3, 48, 128), F32)

        @pl.when(r == peers_r - 1)
        def _():
            ext[s, 15:18] = jnp.zeros((3, 48, 128), F32)

        @pl.when(c == 0)
        def _():
            ext[s, :, 0:8, :] = jnp.zeros((18, 8, 128), F32)

        @pl.when(c == peers_c - 1)
        def _():
            ext[s, :, 40:48, :] = jnp.zeros((18, 8, 128), F32)

        for b in range(7):
            for h in range(2):
                hi, lo = split(ext[s, :, pl.ds(2 * (b + 1) + h, 16, stride=2), :])
                lanes = slice(b * 256 + h * 128, b * 256 + h * 128 + 128)
                shifted[:, 0:16, lanes] = hi
                shifted[:, 16:32, lanes] = lo

        acc[...] = jnp.zeros_like(acc)

        def lag_row(a, carry):
            both = dot(shifted[pl.ds(a, 12)].reshape(384, 1792), whi[a]).reshape(12, 32, 256)
            rest = dot(shifted[pl.ds(a, 12), 0:16, :].reshape(192, 1792), wlo[a])
            acc[...] += (both[:, 0:16] + both[:, 16:32]).reshape(192, 256) + rest
            return carry

        lax.fori_loop(0, 7, lag_row, 0)
        adj[...] += apply_inverse(source() - adj[...] - acc[...])
        if s + 1 < SWEEPS:
            publish(ext.at[s + 1], (slice(3, 15), 8), adj[...])
        else:
            publish(out, (slice(None), 0), adj[...])


def grads_kernel(
    factor, adj, cur, out,
    cg, chi, clo, at, ra, strip, a7h, a7l, acc, terms, gathered, piece, swapped, result,
    cg_send, cg_recv, ra_send, ra_recv, halo_send, halo_recv,
    red_send, red_recv, swap_send, swap_recv, res_send, res_recv, own_sem,
):
    n = 16
    r, c = lax.axis_index("row"), lax.axis_index("col")

    def wrap(x):
        return lax.rem(x + n, n)

    barrier = pltpu.get_barrier_semaphore()

    def greet(k, carry):
        pl.semaphore_signal(barrier, inc=1, device_id=(r, wrap(c + k)), device_id_type=MESH)
        pl.semaphore_signal(barrier, inc=1, device_id=(wrap(r + k), c), device_id_type=MESH)
        return carry

    lax.fori_loop(1, n, greet, 0)

    @pl.when(r != c)
    def _():
        pl.semaphore_signal(barrier, inc=1, device_id=(c, r), device_id_type=MESH)

    for h in range(2):
        part = adj[:, pl.ds(h, 16, stride=2), :].reshape(192, 128)
        part = jnp.concatenate([part, jnp.zeros((64, 128), F32)], axis=0)
        at[h] = part.T.reshape(16, 8, 256)

    own_current = pltpu.make_async_copy(cur, cg.at[c], own_sem.at[0])
    own_current.start()
    own_slice = pltpu.make_async_copy(at.at[:, c], ra.at[c], own_sem.at[1])
    own_slice.start()

    pl.semaphore_wait(barrier, 2 * (n - 1) + jnp.where(r != c, 1, 0))

    def current_copy(k, slot):
        return pltpu.make_async_remote_copy(
            src_ref=cur, dst_ref=cg.at[slot],
            send_sem=cg_send.at[k], recv_sem=cg_recv.at[k],
            device_id=(r, wrap(c + k)), device_id_type=MESH,
        )

    def slice_copy(k, slot):
        return pltpu.make_async_remote_copy(
            src_ref=at.at[:, wrap(c + k)], dst_ref=ra.at[slot],
            send_sem=ra_send.at[k], recv_sem=ra_recv.at[k],
            device_id=(r, wrap(c + k)), device_id_type=MESH,
        )

    def each(first, body):
        def step(k, carry):
            body(k)
            return carry

        lax.fori_loop(first, n, step, 0)

    each(1, lambda k: slice_copy(k, c).start())
    each(1, lambda k: current_copy(k, c).start())

    own_slice.wait()
    each(1, lambda k: slice_copy(k, wrap(c - k)).wait_recv())

    lane = lax.broadcasted_iota(jnp.int32, (16, 128), 1) // 16
    for i in range(12):
        block = slice((i // 8) * 128, (i // 8) * 128 + 128)
        for half in range(2):
            row = jnp.zeros((16, 128), F32)
            for t in range(8):
                x = ra[half * 8 + t, :, :, block].reshape(16, 128)
                shift = ((t - i % 8) * 16) % 128
                if shift:
                    x = pltpu.roll(x, shift, 1)
                row = jnp.where(lane == t, x, row)
            strip[3 + i, :, half * 128:half * 128 + 128] = row

    def edge_copy(d):
        src, dst, to = ((3, 15, wrap(r - 1)), (12, 0, wrap(r + 1)))[d]
        return pltpu.make_async_remote_copy(
            src_ref=strip.at[pl.ds(src, 3)], dst_ref=strip.at[pl.ds(dst, 3)],
            send_sem=halo_send.at[d], recv_sem=halo_recv.at[d],
            device_id=(to, c), device_id_type=MESH,
        )

    for d in range(2):
        edge_copy(d).start()

    column = lax.broadcasted_iota(jnp.int32, (16, 256), 1)

    def spread(e, carry):
        x = strip[e]
        for b in range(7):
            y = x if b == 3 else pltpu.roll(x, (3 - b) % 256, 1)
            if b < 3:
                y = jnp.where(column >= 3 - b, y, 0.0)
            if b > 3:
                y = jnp.where(column < 256 - (b - 3), y, 0.0)
            hi, lo = split(y)
            a7h[e, b * 16:b * 16 + 16, :] = hi
            a7l[e, b * 16:b * 16 + 16, :] = lo
        return carry

    lax.fori_loop(3, 15, spread, 0)

    own_current.wait()
    each(1, lambda k: current_copy(k, wrap(c - k)).wait_recv())

    def convert(t, carry):
        base = pl.multiple_of(t * 16, 16)
        for h in range(2):
            hi, lo = split(cg[t, :, pl.ds(h, 16, stride=2), :])
            chi[:, pl.ds(base, 16), h * 128:h * 128 + 128] = hi
            clo[:, pl.ds(base, 16), h * 128:h * 128 + 128] = lo
        return carry

    lax.fori_loop(0, n, convert, 0)

    acc[...] = jnp.zeros_like(acc)

    def correlate(i, carry):
        high = a7h[pl.ds(i, 7)].reshape(784, 256)
        low = a7l[pl.ds(i, 7)].reshape(784, 256)
        acc[...] += dot(high, chi[i]) + dot(low, chi[i]) + dot(high, clo[i])
        return carry

    lax.fori_loop(3, 9, correlate, 0)
    for d in range(2):
        edge_copy(d).wait_send()
        edge_copy(d).wait_recv()

    @pl.when(r == 0)
    def _():
        strip[0:3] = jnp.zeros((3, 16, 256), F32)

    @pl.when(r == n - 1)
    def _():
        strip[15:18] = jnp.zeros((3, 16, 256), F32)

    lax.fori_loop(0, 3, spread, 0)
    lax.fori_loop(15, 18, spread, 0)
    lax.fori_loop(0, 3, correlate, 0)
    lax.fori_loop(9, 12, correlate, 0)

    for a in range(7):
        x = acc[pl.ds(a * 112, 112), :].reshape(7, 2, 8, 256)
        real = x[:, 0, :, 0:128] + x[:, 1, :, 128:256]
        imag = x[:, 1, :, 0:128] - x[:, 0, :, 128:256]
        terms[a * 7:a * 7 + 7, 0] = real * factor
        terms[a * 7:a * 7 + 7, 1] = imag * factor
    terms[49:56] = jnp.zeros((7, 2, 8, 128), F32)

    def term_piece(p):
        return terms.at[pl.ds(0, 56)].reshape(112, 8, 128).at[pl.ds(p * 7, 7)]

    def reduce_copy(k, slot):
        return pltpu.make_async_remote_copy(
            src_ref=term_piece(wrap(r + k)), dst_ref=gathered.at[slot],
            send_sem=red_send.at[k], recv_sem=red_recv.at[k],
            device_id=(wrap(r + k), c), device_id_type=MESH,
        )

    each(1, lambda k: reduce_copy(k, r).start())
    own_piece = pltpu.make_async_copy(term_piece(r), gathered.at[r], own_sem.at[2])
    own_piece.start()
    own_piece.wait()
    each(1, lambda k: reduce_copy(k, wrap(r - k)).wait_recv())
    total = gathered[0]
    for k in range(1, n):
        total = total + gathered[k]
    piece[...] = total

    def swap_copy():
        return pltpu.make_async_remote_copy(
            src_ref=piece, dst_ref=swapped, send_sem=swap_send, recv_sem=swap_recv,
            device_id=(c, r), device_id_type=MESH,
        )

    @pl.when(r != c)
    def _():
        swap_copy().start()
        swap_copy().wait()

    @pl.when(r == c)
    def _():
        own = pltpu.make_async_copy(piece, swapped, own_sem.at[3])
        own.start()
        own.wait()

    def result_copy(k, slot):
        return pltpu.make_async_remote_copy(
            src_ref=swapped, dst_ref=result.at[pl.ds(slot * 7, 7)],
            send_sem=res_send.at[k], recv_sem=res_recv.at[k],
            device_id=(r, wrap(c + k)), device_id_type=MESH,
        )

    each(1, lambda k: result_copy(k, c).start())
    own_result = pltpu.make_async_copy(swapped, result.at[pl.ds(c * 7, 7)], own_sem.at[4])
    own_result.start()
    own_result.wait()
    each(1, lambda k: result_copy(k, wrap(c - k)).wait_recv())
    out[...] = result[0:98]

    def drain(k):
        slice_copy(k, c).wait_send()
        current_copy(k, c).wait_send()
        reduce_copy(k, r).wait_send()
        result_copy(k, c).wait_send()

    each(1, drain)


def params(collective_id):
    return pltpu.CompilerParams(
        collective_id=collective_id, has_side_effects=True, vmem_limit_bytes=60 * 1024 * 1024
    )


def on_device(adjoint_source, saved_currents, lag_blocks, element_inverse):
    vmem = pl.BlockSpec(memory_space=pltpu.VMEM)
    dma = pltpu.SemaphoreType.DMA
    tile = jax.ShapeDtypeStruct((12, 32, 128), F32)
    adjoint = pl.pallas_call(
        sweeps_kernel,
        out_shape=tile,
        in_specs=[vmem, pl.BlockSpec(memory_space=pl.ANY), vmem],
        out_specs=vmem,
        scratch_shapes=[
            pltpu.VMEM((7, 7, 2, 128, 128), F32),
            pltpu.VMEM((7, 1792, 256), BF16),
            pltpu.VMEM((7, 1792, 256), BF16),
            pltpu.VMEM((256, 256), BF16),
            pltpu.VMEM((256, 256), BF16),
            pltpu.VMEM((SWEEPS, 18, 48, 128), F32),
            pltpu.VMEM((18, 32, 1792), BF16),
            pltpu.VMEM((192, 256), F32),
            pltpu.VMEM((192, 256), F32),
            dma((7,)),
            dma((SWEEPS, 8)),
            dma((SWEEPS, 8)),
        ],
        compiler_params=params(0),
        name="sweeps",
    )(adjoint_source.reshape(12, 32, 128), lag_blocks, element_inverse)

    elements = 12 * lax.axis_size("row") * 16 * lax.axis_size("col")
    factor = -1.0 / math.sqrt(elements)
    lag_grad = pl.pallas_call(
        functools.partial(grads_kernel, factor),
        out_shape=jax.ShapeDtypeStruct((98, 8, 128), F32),
        in_specs=[vmem, vmem],
        out_specs=vmem,
        scratch_shapes=[
            pltpu.VMEM((16, 12, 32, 128), F32),
            pltpu.VMEM((12, 256, 256), BF16),
            pltpu.VMEM((12, 256, 256), BF16),
            pltpu.VMEM((2, 16, 8, 256), F32),
            pltpu.VMEM((16, 2, 8, 256), F32),
            pltpu.VMEM((18, 16, 256), F32),
            pltpu.VMEM((18, 112, 256), BF16),
            pltpu.VMEM((18, 112, 256), BF16),
            pltpu.VMEM((784, 256), F32),
            pltpu.VMEM((56, 2, 8, 128), F32),
            pltpu.VMEM((16, 7, 8, 128), F32),
            pltpu.VMEM((7, 8, 128), F32),
            pltpu.VMEM((7, 8, 128), F32),
            pltpu.VMEM((112, 8, 128), F32),
            dma((16,)), dma((16,)), dma((16,)), dma((16,)), dma((2,)), dma((2,)),
            dma((16,)), dma((16,)), dma(()), dma(()), dma((16,)), dma((16,)), dma((5,)),
        ],
        compiler_params=params(1),
        name="grads",
    )(adjoint, saved_currents.reshape(12, 32, 128))
    return (adjoint.reshape(12, 16, 2, 128), lag_grad.reshape(7, 7, 2, 8, 128))


def solution(mesh):
    return jax.shard_map(
        on_device,
        mesh=mesh,
        in_specs=(P("row", "col", None, None), P("row", "col", None, None), P(), P()),
        out_specs=(P("row", "col", None, None), P(None, None, None, "row", None)),
        check_vma=False,
    )
```

```python
import functools
import math

import jax
import jax.numpy as jnp
from jax import lax
from jax.experimental import pallas as pl
from jax.experimental.pallas import tpu as pltpu
from jax.sharding import PartitionSpec as P

SWEEPS = 2
F32 = jnp.float32
BF16 = jnp.bfloat16
MESH = pl.DeviceIdType.MESH
DIRS = tuple((dr, dc) for dr in (-1, 0, 1) for dc in (-1, 0, 1) if (dr, dc) != (0, 0))


def split(x):
    hi = x.astype(BF16)
    lo = (x - hi.astype(F32)).astype(BF16)
    return hi, lo


def dot(x, y):
    return jnp.dot(x, y, preferred_element_type=F32)


def put_embedded(dst, base, a0, a1):
    dst[pl.ds(base, 128), 0:128] = a0
    dst[pl.ds(base, 128), 128:256] = -a1
    dst[pl.ds(base + 128, 128), 0:128] = a1
    dst[pl.ds(base + 128, 128), 128:256] = a0


def field(ref, rows, start, cols):
    re = ref[rows, pl.ds(start, cols, stride=2), :]
    im = ref[rows, pl.ds(start + 1, cols, stride=2), :]
    return re, im

def kernel(
    factor, src, cur, lag, inv, out, grad,
    stage, whi, wlo, vhi, vlo, ext, shifted, total, adj,
    cg, chi, clo, at, ra, strip, a7h, a7l, terms, gathered, piece, swapped, result,
    lag_sem, send_sem, recv_sem, cg_send, cg_relay, cg_pass, cg_recv,
    ra_send, ra_recv, halo_send, halo_recv, red_send, red_recv,
    swap_send, swap_recv, res_send, res_recv, own_sem,
):
    n = 16
    r, c = lax.axis_index("row"), lax.axis_index("col")

    def wrap(x):
        return lax.rem(x + n, n)

    def lag_copy(a):
        return pltpu.make_async_copy(lag.at[a], stage.at[a], lag_sem.at[a])

    for a in range(7):
        lag_copy(a).start()
    own_current = pltpu.make_async_copy(cur, cg.at[c], own_sem.at[0])
    own_current.start()

    def each(first, body):
        def step(k, carry):
            body(k)
            return carry

        lax.fori_loop(first, n, step, 0)

    barrier = pltpu.get_barrier_semaphore()

    def greet(row, col):
        pl.semaphore_signal(barrier, inc=1, device_id=(row, col), device_id_type=MESH)

    each(1, lambda k: greet(r, wrap(c + k)))
    for dr in (-1, 1):
        for dc in (-1, 0, 1):
            greet(wrap(r + dr), wrap(c + dc))
    each(1, lambda k: greet(wrap(r + k), c))

    @pl.when(r != c)
    def _():
        greet(c, r)

    greetings = 15 + 6 + 15 + jnp.where(r != c, 1, 0)

    def box(dr, dc):
        rows = {-1: (3, 15, 3), 1: (12, 0, 3), 0: (3, 3, 12)}[dr]
        cols = {-1: (8, 40, 8), 1: (32, 0, 8), 0: (8, 8, 32)}[dc]
        return rows, cols

    def halo_copy(s, d):
        dr, dc = DIRS[d]
        (rs, rd, rn), (cs, cd, cn) = box(dr, dc)
        return pltpu.make_async_remote_copy(
            src_ref=ext.at[s, pl.ds(rs, rn), pl.ds(cs, cn), :],
            dst_ref=ext.at[s, pl.ds(rd, rn), pl.ds(cd, cn), :],
            send_sem=send_sem.at[s, d],
            recv_sem=recv_sem.at[s, d],
            device_id=(wrap(r + dr), wrap(c + dc)),
            device_id_type=MESH,
        )

    side, place, core = c // 8, lax.rem(c // 2, 4), lax.rem(c, 2)
    partner = c + 1 - 2 * core
    across = lax.rem(c + 8, n)

    def ring(dx):
        return side * 8 + lax.rem(place + dx, 4) * 2 + core

    def ring_across(dx):
        return lax.rem(ring(dx) + 8, n)

    def current_copy(slot, col, sem):
        return pltpu.make_async_remote_copy(
            src_ref=cg.at[slot], dst_ref=cg.at[slot],
            send_sem=sem, recv_sem=cg_recv.at[slot],
            device_id=(r, col), device_id_type=MESH,
        )

    def own_sends():
        return [current_copy(c, ring(dx), cg_send.at[dx]) for dx in (1, 3, 2)] + [
            current_copy(c, across, cg_send.at[0]),
            current_copy(c, partner, cg_send.at[4]),
        ]

    def relays():
        return [current_copy(across, ring(dx), cg_relay.at[dx]) for dx in (1, 3, 2)]

    def early_passes():
        slots = [ring(1), ring(3), ring(2), across]
        return [current_copy(x, partner, cg_pass.at[k]) for k, x in enumerate(slots)]

    def late_passes():
        slots = [ring_across(1), ring_across(3), ring_across(2)]
        return [current_copy(x, partner, cg_pass.at[4 + k]) for k, x in enumerate(slots)]

    b0h, b0l = split(inv[0])
    b1h, b1l = split(inv[1])
    put_embedded(vhi, 0, b0h, b1h)
    put_embedded(vlo, 0, b0l, b1l)

    def apply_inverse(x):
        xh, xl = split(x)
        return dot(xh, vhi[...]) + dot(xl, vhi[...]) + dot(xh, vlo[...])

    def source():
        re, im = field(src, slice(None), 0, 16)
        return jnp.concatenate([re.reshape(192, 128), im.reshape(192, 128)], axis=1)

    def publish(ref, at_, x):
        rows, start = at_
        ref[rows, pl.ds(start, 16, stride=2), :] = x[:, :128].reshape(12, 16, 128)
        ref[rows, pl.ds(start + 1, 16, stride=2), :] = x[:, 128:].reshape(12, 16, 128)

    adj[...] = apply_inverse(source())
    publish(ext.at[0], (slice(3, 15), 8), adj[...])
    own_current.wait()
    pl.semaphore_wait(barrier, greetings)

    for s in range(SWEEPS):
        for d in range(len(DIRS)):
            halo_copy(s, d).start()
        if s == 0:
            for copy in own_sends():
                copy.start()

            def prepare(a, carry):
                lag_copy(a).wait()

                def one(b, carry):
                    h0, l0 = split(stage[a, b, 0])
                    h1, l1 = split(stage[a, b, 1])
                    base = pl.multiple_of(b * 256, 256)
                    put_embedded(whi.at[a], base, h0, h1)
                    put_embedded(wlo.at[a], base, l0, l1)
                    return carry

                return lax.fori_loop(0, 7, one, carry)

            lax.fori_loop(0, 7, prepare, 0)
        else:
            for copy in early_passes():
                copy.wait_recv()
                copy.start()
            for copy in relays():
                copy.start()
        for d in range(len(DIRS)):
            halo_copy(s, d).wait_recv()

        @pl.when(r == 0)
        def _():
            ext[s, 0:3] = jnp.zeros((3, 48, 128), F32)

        @pl.when(r == n - 1)
        def _():
            ext[s, 15:18] = jnp.zeros((3, 48, 128), F32)

        @pl.when(c == 0)
        def _():
            ext[s, :, 0:8, :] = jnp.zeros((18, 8, 128), F32)

        @pl.when(c == n - 1)
        def _():
            ext[s, :, 40:48, :] = jnp.zeros((18, 8, 128), F32)

        for b in range(7):
            for h in range(2):
                hi, lo = split(ext[s, :, pl.ds(2 * (b + 1) + h, 16, stride=2), :])
                lanes = slice(b * 256 + h * 128, b * 256 + h * 128 + 128)
                shifted[:, 0:16, lanes] = hi
                shifted[:, 16:32, lanes] = lo

        total[...] = jnp.zeros_like(total)

        def lag_row(a, carry):
            both = dot(shifted[pl.ds(a, 12)].reshape(384, 1792), whi[a]).reshape(12, 32, 256)
            rest = dot(shifted[pl.ds(a, 12), 0:16, :].reshape(192, 1792), wlo[a])
            total[...] += (both[:, 0:16] + both[:, 16:32]).reshape(192, 256) + rest
            return carry

        lax.fori_loop(0, 7, lag_row, 0)
        adj[...] += apply_inverse(source() - adj[...] - total[...])
        if s + 1 < SWEEPS:
            publish(ext.at[s + 1], (slice(3, 15), 8), adj[...])

    for h in range(2):
        part = adj[:, h * 128:h * 128 + 128]
        part = jnp.concatenate([part, jnp.zeros((64, 128), F32)], axis=0)
        at[h] = part.T.reshape(16, 8, 256)

    def slice_copy(k, slot):
        return pltpu.make_async_remote_copy(
            src_ref=at.at[:, wrap(c + k)], dst_ref=ra.at[slot],
            send_sem=ra_send.at[k], recv_sem=ra_recv.at[k],
            device_id=(r, wrap(c + k)), device_id_type=MESH,
        )

    each(1, lambda k: slice_copy(k, c).start())
    own_slice = pltpu.make_async_copy(at.at[:, c], ra.at[c], own_sem.at[1])
    own_slice.start()
    publish(out, (slice(None), 0), adj[...])

    for copy in late_passes():
        copy.wait_recv()
        copy.start()

    def convert(t):
        base = pl.multiple_of(t * 16, 16)
        for h in range(2):
            hi, lo = split(cg[t, :, pl.ds(h, 16, stride=2), :])
            chi[:, pl.ds(base, 16), h * 128:h * 128 + 128] = hi
            clo[:, pl.ds(base, 16), h * 128:h * 128 + 128] = lo

    for dx in range(4):
        other = ring(dx) + 1 - 2 * core
        current_copy(other, partner, cg_send.at[4]).wait_recv()
        current_copy(lax.rem(other + 8, n), partner, cg_send.at[4]).wait_recv()
    lax.fori_loop(0, n, lambda t, carry: (convert(t), carry)[1], 0)

    own_slice.wait()
    each(1, lambda k: slice_copy(k, wrap(c - k)).wait_recv())

    lane = lax.broadcasted_iota(jnp.int32, (16, 128), 1) // 16
    for i in range(12):
        block = slice((i // 8) * 128, (i // 8) * 128 + 128)
        for half in range(2):
            row = jnp.zeros((16, 128), F32)
            for t in range(8):
                x = ra[half * 8 + t, :, :, block].reshape(16, 128)
                shift = ((t - i % 8) * 16) % 128
                if shift:
                    x = pltpu.roll(x, shift, 1)
                row = jnp.where(lane == t, x, row)
            strip[3 + i, :, half * 128:half * 128 + 128] = row

    def edge_copy(d):
        src_, dst, to = ((3, 15, wrap(r - 1)), (12, 0, wrap(r + 1)))[d]
        return pltpu.make_async_remote_copy(
            src_ref=strip.at[pl.ds(src_, 3)], dst_ref=strip.at[pl.ds(dst, 3)],
            send_sem=halo_send.at[d], recv_sem=halo_recv.at[d],
            device_id=(to, c), device_id_type=MESH,
        )

    for d in range(2):
        edge_copy(d).start()

    column = lax.broadcasted_iota(jnp.int32, (16, 256), 1)

    def spread(e, carry):
        x = strip[e]
        for b in range(7):
            y = x if b == 3 else pltpu.roll(x, (3 - b) % 256, 1)
            if b < 3:
                y = jnp.where(column >= 3 - b, y, 0.0)
            if b > 3:
                y = jnp.where(column < 256 - (b - 3), y, 0.0)
            hi, lo = split(y)
            a7h[e, b * 16:b * 16 + 16, :] = hi
            a7l[e, b * 16:b * 16 + 16, :] = lo
        return carry

    lax.fori_loop(3, 15, spread, 0)
    for d in range(2):
        edge_copy(d).wait_recv()

    @pl.when(r == 0)
    def _():
        strip[0:3] = jnp.zeros((3, 16, 256), F32)

    @pl.when(r == n - 1)
    def _():
        strip[15:18] = jnp.zeros((3, 16, 256), F32)

    lax.fori_loop(0, 3, spread, 0)
    lax.fori_loop(15, 18, spread, 0)

    def reduce_copy(p, slot):
        return pltpu.make_async_remote_copy(
            src_ref=terms.at[p], dst_ref=gathered.at[slot],
            send_sem=red_send.at[p], recv_sem=red_recv.at[slot],
            device_id=(p, c), device_id_type=MESH,
        )

    def keep_copy():
        return pltpu.make_async_copy(terms.at[r], gathered.at[r], own_sem.at[2])

    def correlate(a, carry):
        high = jnp.concatenate([a7h[a + i] for i in range(12)], axis=1)
        low = jnp.concatenate([a7l[a + i] for i in range(12)], axis=1)
        both = dot(jnp.concatenate([high, low], axis=0), chi[...].reshape(3072, 256))
        rest = dot(high, clo[...].reshape(3072, 256))
        x = (both[0:112] + both[112:224] + rest).reshape(7, 2, 8, 256)
        real = (x[:, 0, :, 0:128] + x[:, 1, :, 128:256]) * factor
        imag = (x[:, 1, :, 0:128] - x[:, 0, :, 128:256]) * factor
        for b in range(7):
            for h, part in ((0, real), (1, imag)):
                tile = b * 2 + h
                terms[a * 2 + tile // 7, tile % 7] = part[b]
        for e in range(2):
            p = a * 2 + e

            @pl.when(p != r)
            def _():
                reduce_copy(p, r).start()

            @pl.when(p == r)
            def _():
                keep_copy().start()

        return carry

    lax.fori_loop(0, 7, correlate, 0)

    @pl.when(r < 14)
    def _():
        def collect(k, carry):
            @pl.when(k == r)
            def _():
                keep_copy().wait()

            @pl.when(k != r)
            def _():
                reduce_copy(r, k).wait_recv()

            return carry

        lax.fori_loop(0, n, collect, 0)
        x = gathered[0]
        for k in range(1, n):
            x = x + gathered[k]
        piece[...] = x

    def swap_copy():
        return pltpu.make_async_remote_copy(
            src_ref=piece, dst_ref=swapped, send_sem=swap_send, recv_sem=swap_recv,
            device_id=(c, r), device_id_type=MESH,
        )

    @pl.when(jnp.logical_and(r != c, r < 14))
    def _():
        swap_copy().start()

    @pl.when(jnp.logical_and(r != c, c < 14))
    def _():
        swap_copy().wait_recv()

    @pl.when(jnp.logical_and(r == c, r < 14))
    def _():
        own = pltpu.make_async_copy(piece, swapped, own_sem.at[3])
        own.start()
        own.wait()

    @pl.when(jnp.logical_and(r != c, r < 14))
    def _():
        swap_copy().wait_send()

    def result_copy(k, slot):
        return pltpu.make_async_remote_copy(
            src_ref=swapped, dst_ref=result.at[slot],
            send_sem=res_send.at[k], recv_sem=res_recv.at[slot],
            device_id=(r, wrap(c + k)), device_id_type=MESH,
        )

    own_result = pltpu.make_async_copy(swapped, result.at[c], own_sem.at[4])

    @pl.when(c < 14)
    def _():
        each(1, lambda k: result_copy(k, c).start())
        own_result.start()

    def drain_reduce(p, carry):
        @pl.when(p != r)
        def _():
            reduce_copy(p, r).wait_send()

        return carry

    lax.fori_loop(0, 14, drain_reduce, 0)
    each(1, lambda k: slice_copy(k, c).wait_send())
    for copy in own_sends() + relays() + early_passes() + late_passes():
        copy.wait_send()
    for d in range(2):
        edge_copy(d).wait_send()
    for s in range(SWEEPS):
        for d in range(len(DIRS)):
            halo_copy(s, d).wait_send()

    def finish(p, carry):
        @pl.when(p == c)
        def _():
            own_result.wait()

        @pl.when(p != c)
        def _():
            result_copy(1, p).wait_recv()

        return carry

    lax.fori_loop(0, 14, finish, 0)
    grad[...] = result[0:14].reshape(98, 8, 128)

    @pl.when(c < 14)
    def _():
        each(1, lambda k: result_copy(k, c).wait_send())


def on_device(adjoint_source, saved_currents, lag_blocks, element_inverse):
    vmem = pl.BlockSpec(memory_space=pltpu.VMEM)
    hbm = pl.BlockSpec(memory_space=pl.ANY)
    dma = pltpu.SemaphoreType.DMA
    elements = 12 * lax.axis_size("row") * 16 * lax.axis_size("col")
    adjoint, lag_grad = pl.pallas_call(
        functools.partial(kernel, -1.0 / math.sqrt(elements)),
        out_shape=(
            jax.ShapeDtypeStruct((12, 32, 128), F32),
            jax.ShapeDtypeStruct((98, 8, 128), F32),
        ),
        in_specs=[vmem, hbm, hbm, vmem],
        out_specs=(vmem, vmem),
        scratch_shapes=[
            pltpu.VMEM((7, 7, 2, 128, 128), F32),
            pltpu.VMEM((7, 1792, 256), BF16),
            pltpu.VMEM((7, 1792, 256), BF16),
            pltpu.VMEM((256, 256), BF16),
            pltpu.VMEM((256, 256), BF16),
            pltpu.VMEM((SWEEPS, 18, 48, 128), F32),
            pltpu.VMEM((18, 32, 1792), BF16),
            pltpu.VMEM((192, 256), F32),
            pltpu.VMEM((192, 256), F32),
            pltpu.VMEM((16, 12, 32, 128), F32),
            pltpu.VMEM((12, 256, 256), BF16),
            pltpu.VMEM((12, 256, 256), BF16),
            pltpu.VMEM((2, 16, 8, 256), F32),
            pltpu.VMEM((16, 2, 8, 256), F32),
            pltpu.VMEM((18, 16, 256), F32),
            pltpu.VMEM((18, 112, 256), BF16),
            pltpu.VMEM((18, 112, 256), BF16),
            pltpu.VMEM((14, 7, 8, 128), F32),
            pltpu.VMEM((16, 7, 8, 128), F32),
            pltpu.VMEM((7, 8, 128), F32),
            pltpu.VMEM((7, 8, 128), F32),
            pltpu.VMEM((16, 7, 8, 128), F32),
            dma((7,)), dma((SWEEPS, 8)), dma((SWEEPS, 8)),
            dma((5,)), dma((4,)), dma((7,)), dma((16,)),
            dma((16,)), dma((16,)), dma((2,)), dma((2,)),
            dma((16,)), dma((16,)), dma(()), dma(()), dma((16,)), dma((16,)), dma((5,)),
        ],
        compiler_params=pltpu.CompilerParams(
            collective_id=0, has_side_effects=True, vmem_limit_bytes=62 * 1024 * 1024
        ),
        name="adjoint_gradient",
    )(
        adjoint_source.reshape(12, 32, 128),
        saved_currents.reshape(12, 32, 128),
        lag_blocks,
        element_inverse,
    )
    return (adjoint.reshape(12, 16, 2, 128), lag_grad.reshape(7, 7, 2, 8, 128))


def solution(mesh):
    return jax.shard_map(
        on_device,
        mesh=mesh,
        in_specs=(P("row", "col", None, None), P("row", "col", None, None), P(), P()),
        out_specs=(P("row", "col", None, None), P(None, None, None, "row", None)),
        check_vma=False,
    )
```

```python
import functools
import math

import jax
import jax.numpy as jnp
from jax import lax
from jax.experimental import pallas as pl
from jax.experimental.pallas import tpu as pltpu
from jax.sharding import PartitionSpec as P

SWEEPS = 2
F32 = jnp.float32
BF16 = jnp.bfloat16
MESH = pl.DeviceIdType.MESH
DIRS = tuple((dr, dc) for dr in (-1, 0, 1) for dc in (-1, 0, 1) if (dr, dc) != (0, 0))


def split(x):
    hi = x.astype(BF16)
    lo = (x - hi.astype(F32)).astype(BF16)
    return hi, lo


def dot(x, y):
    return jnp.dot(x, y, preferred_element_type=F32)


def put_embedded(dst, base, a0, a1):
    dst[pl.ds(base, 128), 0:128] = a0
    dst[pl.ds(base, 128), 128:256] = -a1
    dst[pl.ds(base + 128, 128), 0:128] = a1
    dst[pl.ds(base + 128, 128), 128:256] = a0


def field(ref, rows, start, cols):
    re = ref[rows, pl.ds(start, cols, stride=2), :]
    im = ref[rows, pl.ds(start + 1, cols, stride=2), :]
    return re, im

def kernel(
    factor, src_hbm, cur, lag, inv_hbm, out, grad,
    src, inv, stage, whi, wlo, vhi, vlo, ext, near_hi, near_lo, total, adj,
    cg, chi, clo, at, ra, strip, a7h, a7l, terms, gathered, piece, swapped, result,
    lag_sem, send_sem, recv_sem, cg_send, cg_relay, cg_pass, cg_recv,
    ra_send, ra_recv, halo_send, halo_recv, red_send, red_recv,
    swap_send, swap_recv, res_send, res_recv, own_sem,
):
    n = 16
    r, c = lax.axis_index("row"), lax.axis_index("col")

    def wrap(x):
        return lax.rem(x + n, n)

    src_copy = pltpu.make_async_copy(src_hbm, src, own_sem.at[5])
    inv_copy = pltpu.make_async_copy(inv_hbm, inv, own_sem.at[6])
    src_copy.start()
    inv_copy.start()

    def lag_copy(a):
        return pltpu.make_async_copy(lag.at[a], stage.at[a], lag_sem.at[a])

    for a in range(7):
        lag_copy(a).start()
    own_current = pltpu.make_async_copy(cur, cg.at[c], own_sem.at[0])
    own_current.start()

    def each(first, body):
        def step(k, carry):
            body(k)
            return carry

        lax.fori_loop(first, n, step, 0)

    barrier = pltpu.get_barrier_semaphore()

    def greet(row, col):
        pl.semaphore_signal(barrier, inc=1, device_id=(row, col), device_id_type=MESH)

    each(1, lambda k: greet(r, wrap(c + k)))
    for dr in (-1, 1):
        for dc in (-1, 0, 1):
            greet(wrap(r + dr), wrap(c + dc))
    each(1, lambda k: greet(wrap(r + k), c))

    @pl.when(r != c)
    def _():
        greet(c, r)

    greetings = 15 + 6 + 15 + jnp.where(r != c, 1, 0)

    def box(dr, dc):
        rows = {-1: (3, 15, 3), 1: (12, 0, 3), 0: (3, 3, 12)}[dr]
        cols = {-1: (8, 40, 8), 1: (32, 0, 8), 0: (8, 8, 32)}[dc]
        return rows, cols

    def halo_copy(s, d):
        dr, dc = DIRS[d]
        (rs, rd, rn), (cs, cd, cn) = box(dr, dc)
        return pltpu.make_async_remote_copy(
            src_ref=ext.at[s, pl.ds(rs, rn), pl.ds(cs, cn), :],
            dst_ref=ext.at[s, pl.ds(rd, rn), pl.ds(cd, cn), :],
            send_sem=send_sem.at[s, d],
            recv_sem=recv_sem.at[s, d],
            device_id=(wrap(r + dr), wrap(c + dc)),
            device_id_type=MESH,
        )

    side, place, core = c // 8, lax.rem(c // 2, 4), lax.rem(c, 2)
    partner = c + 1 - 2 * core
    across = lax.rem(c + 8, n)

    def ring(dx):
        return side * 8 + lax.rem(place + dx, 4) * 2 + core

    def ring_across(dx):
        return lax.rem(ring(dx) + 8, n)

    def current_copy(slot, col, sem):
        return pltpu.make_async_remote_copy(
            src_ref=cg.at[slot], dst_ref=cg.at[slot],
            send_sem=sem, recv_sem=cg_recv.at[slot],
            device_id=(r, col), device_id_type=MESH,
        )

    def own_sends():
        return [current_copy(c, ring(dx), cg_send.at[dx]) for dx in (1, 3, 2)] + [
            current_copy(c, across, cg_send.at[0]),
            current_copy(c, partner, cg_send.at[4]),
        ]

    def relays():
        return [current_copy(across, ring(dx), cg_relay.at[dx]) for dx in (1, 3, 2)]

    def early_passes():
        slots = [ring(1), ring(3), ring(2), across]
        return [current_copy(x, partner, cg_pass.at[k]) for k, x in enumerate(slots)]

    def late_passes():
        slots = [ring_across(1), ring_across(3), ring_across(2)]
        return [current_copy(x, partner, cg_pass.at[4 + k]) for k, x in enumerate(slots)]

    inv_copy.wait()
    src_copy.wait()
    b0h, b0l = split(inv[0])
    b1h, b1l = split(inv[1])
    put_embedded(vhi, 0, b0h, b1h)
    put_embedded(vlo, 0, b0l, b1l)

    def apply_inverse(x):
        xh, xl = split(x)
        return dot(xh, vhi[...]) + dot(xl, vhi[...]) + dot(xh, vlo[...])

    def source():
        re, im = field(src, slice(None), 0, 16)
        return jnp.concatenate([re.reshape(192, 128), im.reshape(192, 128)], axis=1)

    def publish(ref, at_, x):
        rows, start = at_
        ref[rows, pl.ds(start, 16, stride=2), :] = x[:, :128].reshape(12, 16, 128)
        ref[rows, pl.ds(start + 1, 16, stride=2), :] = x[:, 128:].reshape(12, 16, 128)

    adj[...] = apply_inverse(source())
    publish(ext.at[0], (slice(3, 15), 8), adj[...])
    own_current.wait()
    pl.semaphore_wait(barrier, greetings)

    def sweep(s, carry):
        for d in range(len(DIRS)):
            halo_copy(s, d).start()
        @pl.when(s == 0)
        def _():
            for copy in own_sends():
                copy.start()

            def prepare(a, carry):
                lag_copy(a).wait()

                def one(b, carry):
                    h0, l0 = split(stage[a, b, 0])
                    h1, l1 = split(stage[a, b, 1])
                    base = pl.multiple_of(b * 256, 256)
                    put_embedded(whi.at[a], base, h0, h1)
                    put_embedded(wlo.at[a], base, l0, l1)
                    return carry

                return lax.fori_loop(0, 7, one, carry)

            lax.fori_loop(0, 7, prepare, 0)

        @pl.when(s > 0)
        def _():
            for copy in early_passes():
                copy.wait_recv()
                copy.start()
            for copy in relays():
                copy.start()

        for d in range(len(DIRS)):
            halo_copy(s, d).wait_recv()

        @pl.when(r == 0)
        def _():
            ext[s, 0:3] = jnp.zeros((3, 48, 128), F32)

        @pl.when(r == n - 1)
        def _():
            ext[s, 15:18] = jnp.zeros((3, 48, 128), F32)

        @pl.when(c == 0)
        def _():
            ext[s, :, 0:8, :] = jnp.zeros((18, 8, 128), F32)

        @pl.when(c == n - 1)
        def _():
            ext[s, :, 40:48, :] = jnp.zeros((18, 8, 128), F32)

        for b in range(7):
            for h in range(2):
                hi, lo = split(ext[s, :, pl.ds(2 * (b + 1) + h, 16, stride=2), :])
                lanes = slice(b * 256 + h * 128, b * 256 + h * 128 + 128)
                near_hi[:, :, lanes] = hi
                near_lo[:, :, lanes] = lo

        total[...] = jnp.zeros_like(total)

        def lag_row(a, carry):
            hi = near_hi[pl.ds(a, 12)].reshape(192, 1792)
            lo = near_lo[pl.ds(a, 12)].reshape(192, 1792)
            total[...] += dot(hi, whi[a]) + dot(lo, whi[a]) + dot(hi, wlo[a])
            return carry

        lax.fori_loop(0, 7, lag_row, 0)
        adj[...] += apply_inverse(source() - adj[...] - total[...])
        @pl.when(s + 1 < SWEEPS)
        def _():
            publish(ext.at[lax.rem(s + 1, SWEEPS)], (slice(3, 15), 8), adj[...])

        return carry

    lax.fori_loop(0, SWEEPS, sweep, 0)

    for h in range(2):
        part = adj[:, h * 128:h * 128 + 128]
        part = jnp.concatenate([part, jnp.zeros((64, 128), F32)], axis=0)
        at[h] = part.T.reshape(16, 8, 256)

    def slice_copy(k, slot):
        return pltpu.make_async_remote_copy(
            src_ref=at.at[:, wrap(c + k)], dst_ref=ra.at[slot],
            send_sem=ra_send.at[k], recv_sem=ra_recv.at[k],
            device_id=(r, wrap(c + k)), device_id_type=MESH,
        )

    each(1, lambda k: slice_copy(k, c).start())
    own_slice = pltpu.make_async_copy(at.at[:, c], ra.at[c], own_sem.at[1])
    own_slice.start()
    publish(out, (slice(None), 0), adj[...])

    for copy in late_passes():
        copy.wait_recv()
        copy.start()

    def convert(t):
        base = pl.multiple_of(t * 16, 16)
        for h in range(2):
            hi, lo = split(cg[t, :, pl.ds(h, 16, stride=2), :])
            chi[:, pl.ds(base, 16), h * 128:h * 128 + 128] = hi
            clo[:, pl.ds(base, 16), h * 128:h * 128 + 128] = lo

    for dx in range(4):
        other = ring(dx) + 1 - 2 * core
        current_copy(other, partner, cg_send.at[4]).wait_recv()
        current_copy(lax.rem(other + 8, n), partner, cg_send.at[4]).wait_recv()
    lax.fori_loop(0, n, lambda t, carry: (convert(t), carry)[1], 0)

    own_slice.wait()
    each(1, lambda k: slice_copy(k, wrap(c - k)).wait_recv())

    lane = lax.broadcasted_iota(jnp.int32, (16, 128), 1) // 16
    for i in range(12):
        block = slice((i // 8) * 128, (i // 8) * 128 + 128)
        for half in range(2):
            row = jnp.zeros((16, 128), F32)
            for t in range(8):
                x = ra[half * 8 + t, :, :, block].reshape(16, 128)
                shift = ((t - i % 8) * 16) % 128
                if shift:
                    x = pltpu.roll(x, shift, 1)
                row = jnp.where(lane == t, x, row)
            strip[3 + i, :, half * 128:half * 128 + 128] = row

    def edge_copy(d):
        src_, dst, to = ((3, 15, wrap(r - 1)), (12, 0, wrap(r + 1)))[d]
        return pltpu.make_async_remote_copy(
            src_ref=strip.at[pl.ds(src_, 3)], dst_ref=strip.at[pl.ds(dst, 3)],
            send_sem=halo_send.at[d], recv_sem=halo_recv.at[d],
            device_id=(to, c), device_id_type=MESH,
        )

    for d in range(2):
        edge_copy(d).start()

    column = lax.broadcasted_iota(jnp.int32, (16, 256), 1)

    def spread(e, carry):
        x = strip[e]
        for b in range(7):
            y = x if b == 3 else pltpu.roll(x, (3 - b) % 256, 1)
            if b < 3:
                y = jnp.where(column >= 3 - b, y, 0.0)
            if b > 3:
                y = jnp.where(column < 256 - (b - 3), y, 0.0)
            hi, lo = split(y)
            a7h[e, b * 16:b * 16 + 16, :] = hi
            a7l[e, b * 16:b * 16 + 16, :] = lo
        return carry

    lax.fori_loop(3, 15, spread, 0)
    for d in range(2):
        edge_copy(d).wait_recv()

    @pl.when(r == 0)
    def _():
        strip[0:3] = jnp.zeros((3, 16, 256), F32)

    @pl.when(r == n - 1)
    def _():
        strip[15:18] = jnp.zeros((3, 16, 256), F32)

    lax.fori_loop(0, 3, spread, 0)
    lax.fori_loop(15, 18, spread, 0)

    def reduce_copy(p, slot):
        return pltpu.make_async_remote_copy(
            src_ref=terms.at[p], dst_ref=gathered.at[slot],
            send_sem=red_send.at[p], recv_sem=red_recv.at[slot],
            device_id=(p, c), device_id_type=MESH,
        )

    def keep_copy():
        return pltpu.make_async_copy(terms.at[r], gathered.at[r], own_sem.at[2])

    def correlate(a, carry):
        high = jnp.concatenate([a7h[a + i] for i in range(12)], axis=1)
        low = jnp.concatenate([a7l[a + i] for i in range(12)], axis=1)
        both = dot(jnp.concatenate([high, low], axis=0), chi[...].reshape(3072, 256))
        rest = dot(high, clo[...].reshape(3072, 256))
        x = (both[0:112] + both[112:224] + rest).reshape(7, 2, 8, 256)
        real = (x[:, 0, :, 0:128] + x[:, 1, :, 128:256]) * factor
        imag = (x[:, 1, :, 0:128] - x[:, 0, :, 128:256]) * factor
        for b in range(7):
            for h, part in ((0, real), (1, imag)):
                tile = b * 2 + h
                terms[a * 2 + tile // 7, tile % 7] = part[b]
        for e in range(2):
            p = a * 2 + e

            @pl.when(p != r)
            def _():
                reduce_copy(p, r).start()

            @pl.when(p == r)
            def _():
                keep_copy().start()

        return carry

    lax.fori_loop(0, 7, correlate, 0)

    @pl.when(r < 14)
    def _():
        def collect(k, carry):
            @pl.when(k == r)
            def _():
                keep_copy().wait()

            @pl.when(k != r)
            def _():
                reduce_copy(r, k).wait_recv()

            return carry

        lax.fori_loop(0, n, collect, 0)
        x = gathered[0]
        for k in range(1, n):
            x = x + gathered[k]
        piece[...] = x

    def swap_copy():
        return pltpu.make_async_remote_copy(
            src_ref=piece, dst_ref=swapped, send_sem=swap_send, recv_sem=swap_recv,
            device_id=(c, r), device_id_type=MESH,
        )

    @pl.when(jnp.logical_and(r != c, r < 14))
    def _():
        swap_copy().start()

    @pl.when(jnp.logical_and(r != c, c < 14))
    def _():
        swap_copy().wait_recv()

    @pl.when(jnp.logical_and(r == c, r < 14))
    def _():
        own = pltpu.make_async_copy(piece, swapped, own_sem.at[3])
        own.start()
        own.wait()

    @pl.when(jnp.logical_and(r != c, r < 14))
    def _():
        swap_copy().wait_send()

    def result_copy(k, slot):
        return pltpu.make_async_remote_copy(
            src_ref=swapped, dst_ref=result.at[slot],
            send_sem=res_send.at[k], recv_sem=res_recv.at[slot],
            device_id=(r, wrap(c + k)), device_id_type=MESH,
        )

    own_result = pltpu.make_async_copy(swapped, result.at[c], own_sem.at[4])

    @pl.when(c < 14)
    def _():
        each(1, lambda k: result_copy(k, c).start())
        own_result.start()

    def drain_reduce(p, carry):
        @pl.when(p != r)
        def _():
            reduce_copy(p, r).wait_send()

        return carry

    lax.fori_loop(0, 14, drain_reduce, 0)
    each(1, lambda k: slice_copy(k, c).wait_send())
    for copy in own_sends() + relays() + early_passes() + late_passes():
        copy.wait_send()
    for d in range(2):
        edge_copy(d).wait_send()
    for s in range(SWEEPS):
        for d in range(len(DIRS)):
            halo_copy(s, d).wait_send()

    def finish(p, carry):
        @pl.when(p == c)
        def _():
            own_result.wait()

        @pl.when(p != c)
        def _():
            result_copy(1, p).wait_recv()

        return carry

    lax.fori_loop(0, 14, finish, 0)
    grad[...] = result[0:14].reshape(98, 8, 128)

    @pl.when(c < 14)
    def _():
        each(1, lambda k: result_copy(k, c).wait_send())


def hand_out(adj, grad, adj_out, grad_out, adj_buf, grad_buf, sem):
    into = [
        pltpu.make_async_copy(adj, adj_buf, sem.at[0]),
        pltpu.make_async_copy(grad, grad_buf, sem.at[1]),
    ]
    back = [
        pltpu.make_async_copy(adj_buf, adj_out, sem.at[2]),
        pltpu.make_async_copy(grad_buf, grad_out, sem.at[3]),
    ]
    for copy in into:
        copy.start()
    for first, second in zip(into, back):
        first.wait()
        second.start()
    for copy in back:
        copy.wait()


def on_device(adjoint_source, saved_currents, lag_blocks, element_inverse):
    vmem = pl.BlockSpec(memory_space=pltpu.VMEM)
    hbm = pl.BlockSpec(memory_space=pl.ANY)
    dma = pltpu.SemaphoreType.DMA
    elements = 12 * lax.axis_size("row") * 16 * lax.axis_size("col")
    adjoint, lag_grad = pl.pallas_call(
        functools.partial(kernel, -1.0 / math.sqrt(elements)),
        out_shape=(
            jax.ShapeDtypeStruct((12, 32, 128), F32),
            jax.ShapeDtypeStruct((98, 8, 128), F32),
        ),
        in_specs=[pl.BlockSpec(memory_space=pltpu.HBM)] * 4,
        out_specs=(vmem, vmem),
        scratch_shapes=[
            pltpu.VMEM((12, 32, 128), F32),
            pltpu.VMEM((2, 128, 128), F32),
            pltpu.VMEM((7, 7, 2, 128, 128), F32),
            pltpu.VMEM((7, 1792, 256), BF16),
            pltpu.VMEM((7, 1792, 256), BF16),
            pltpu.VMEM((256, 256), BF16),
            pltpu.VMEM((256, 256), BF16),
            pltpu.VMEM((SWEEPS, 18, 48, 128), F32),
            pltpu.VMEM((18, 16, 1792), BF16),
            pltpu.VMEM((18, 16, 1792), BF16),
            pltpu.VMEM((192, 256), F32),
            pltpu.VMEM((192, 256), F32),
            pltpu.VMEM((16, 12, 32, 128), F32),
            pltpu.VMEM((12, 256, 256), BF16),
            pltpu.VMEM((12, 256, 256), BF16),
            pltpu.VMEM((2, 16, 8, 256), F32),
            pltpu.VMEM((16, 2, 8, 256), F32),
            pltpu.VMEM((18, 16, 256), F32),
            pltpu.VMEM((18, 112, 256), BF16),
            pltpu.VMEM((18, 112, 256), BF16),
            pltpu.VMEM((14, 7, 8, 128), F32),
            pltpu.VMEM((16, 7, 8, 128), F32),
            pltpu.VMEM((7, 8, 128), F32),
            pltpu.VMEM((7, 8, 128), F32),
            pltpu.VMEM((16, 7, 8, 128), F32),
            dma((7,)), dma((SWEEPS, 8)), dma((SWEEPS, 8)),
            dma((5,)), dma((4,)), dma((7,)), dma((16,)),
            dma((16,)), dma((16,)), dma((2,)), dma((2,)),
            dma((16,)), dma((16,)), dma(()), dma(()), dma((16,)), dma((16,)), dma((7,)),
        ],
        compiler_params=pltpu.CompilerParams(
            collective_id=0, has_side_effects=True, vmem_limit_bytes=62 * 1024 * 1024
        ),
        name="adjoint_gradient",
    )(
        adjoint_source.reshape(12, 32, 128),
        saved_currents.reshape(12, 32, 128),
        lag_blocks,
        element_inverse,
    )
    adjoint, lag_grad = pl.pallas_call(
        hand_out,
        out_shape=(
            jax.ShapeDtypeStruct((12, 32, 128), F32),
            jax.ShapeDtypeStruct((98, 8, 128), F32),
        ),
        in_specs=[hbm, hbm],
        out_specs=(hbm, hbm),
        scratch_shapes=[
            pltpu.VMEM((12, 32, 128), F32), pltpu.VMEM((98, 8, 128), F32), dma((4,)),
        ],
        compiler_params=pltpu.CompilerParams(vmem_limit_bytes=62 * 1024 * 1024),
        name="hand_out",
    )(adjoint, lag_grad)
    return (adjoint.reshape(12, 16, 2, 128), lag_grad.reshape(7, 7, 2, 8, 128))


def solution(mesh):
    return jax.shard_map(
        on_device,
        mesh=mesh,
        in_specs=(P("row", "col", None, None), P("row", "col", None, None), P(), P()),
        out_specs=(P("row", "col", None, None), P(None, None, None, "row", None)),
        check_vma=False,
    )
```

```python
import functools
import math

import jax
import jax.numpy as jnp
from jax import lax
from jax.experimental import pallas as pl
from jax.experimental.pallas import tpu as pltpu
from jax.sharding import PartitionSpec as P

SWEEPS = 2
F32 = jnp.float32
BF16 = jnp.bfloat16
MESH = pl.DeviceIdType.MESH
DIRS = ((-1, -1), (-1, 1), (1, -1), (1, 1), (0, -1), (0, 1), (-1, 0), (1, 0))
SIDES = (4, 5)
REST = (0, 1, 2, 3, 6, 7)


def split(x):
    hi = x.astype(BF16)
    lo = (x - hi.astype(F32)).astype(BF16)
    return hi, lo


def dot(x, y):
    return jnp.dot(x, y, preferred_element_type=F32)


def put_embedded(dst, base, a0, a1):
    dst[pl.ds(base, 128), 0:128] = a0
    dst[pl.ds(base, 128), 128:256] = -a1
    dst[pl.ds(base + 128, 128), 0:128] = a1
    dst[pl.ds(base + 128, 128), 128:256] = a0


def field(ref, rows, start, cols):
    re = ref[rows, pl.ds(start, cols, stride=2), :]
    im = ref[rows, pl.ds(start + 1, cols, stride=2), :]
    return re, im

def kernel(
    factor, src_hbm, cur, lag, inv_hbm, out, grad,
    src, inv, stage, whi, wlo, vhi, vlo, ext, near_hi, near_lo, total, adj,
    cg, chi, clo, at, ra, strip, a7h, a7l, terms, gathered, piece, swapped, result,
    lag_sem, send_sem, recv_sem, cg_send, cg_relay, cg_pass, cg_recv,
    ra_send, ra_recv, halo_send, halo_recv, red_send, red_recv,
    swap_send, swap_recv, res_send, res_recv, own_sem,
):
    n = 16
    r, c = lax.axis_index("row"), lax.axis_index("col")

    def wrap(x):
        return lax.rem(x + n, n)

    src_copy = pltpu.make_async_copy(src_hbm, src, own_sem.at[5])
    inv_copy = pltpu.make_async_copy(inv_hbm, inv, own_sem.at[6])
    src_copy.start()
    inv_copy.start()

    def lag_copy(a):
        return pltpu.make_async_copy(lag.at[a], stage.at[a], lag_sem.at[a])

    for a in range(7):
        lag_copy(a).start()
    own_current = pltpu.make_async_copy(cur, cg.at[c], own_sem.at[0])
    own_current.start()

    def each(first, body):
        def step(k, carry):
            body(k)
            return carry

        lax.fori_loop(first, n, step, 0)

    barrier = pltpu.get_barrier_semaphore()

    def greet(row, col):
        pl.semaphore_signal(barrier, inc=1, device_id=(row, col), device_id_type=MESH)

    each(1, lambda k: greet(r, wrap(c + k)))
    for dr in (-1, 1):
        for dc in (-1, 0, 1):
            greet(wrap(r + dr), wrap(c + dc))
    each(1, lambda k: greet(wrap(r + k), c))

    @pl.when(r != c)
    def _():
        greet(c, r)

    greetings = 15 + 6 + 15 + jnp.where(r != c, 1, 0)

    def box(dr, dc):
        rows = {-1: (3, 15, 3), 1: (12, 0, 3), 0: (3, 3, 12)}[dr]
        cols = {-1: (8, 40, 8), 1: (32, 0, 8), 0: (8, 8, 32)}[dc]
        return rows, cols

    def halo_copy(s, d):
        dr, dc = DIRS[d]
        (rs, rd, rn), (cs, cd, cn) = box(dr, dc)
        return pltpu.make_async_remote_copy(
            src_ref=ext.at[s, pl.ds(rs, rn), pl.ds(cs, cn), :],
            dst_ref=ext.at[s, pl.ds(rd, rn), pl.ds(cd, cn), :],
            send_sem=send_sem.at[s, d],
            recv_sem=recv_sem.at[s, d],
            device_id=(wrap(r + dr), wrap(c + dc)),
            device_id_type=MESH,
        )

    side, place, core = c // 8, lax.rem(c // 2, 4), lax.rem(c, 2)
    partner = c + 1 - 2 * core
    across = lax.rem(c + 8, n)

    def ring(dx):
        return side * 8 + lax.rem(place + dx, 4) * 2 + core

    def ring_across(dx):
        return lax.rem(ring(dx) + 8, n)

    def current_copy(slot, col, sem):
        return pltpu.make_async_remote_copy(
            src_ref=cg.at[slot], dst_ref=cg.at[slot],
            send_sem=sem, recv_sem=cg_recv.at[slot],
            device_id=(r, col), device_id_type=MESH,
        )

    def own_sends():
        return [current_copy(c, ring(dx), cg_send.at[dx]) for dx in (1, 3, 2)] + [
            current_copy(c, across, cg_send.at[0]),
            current_copy(c, partner, cg_send.at[4]),
        ]

    def relays():
        return [current_copy(across, ring(dx), cg_relay.at[dx]) for dx in (1, 3, 2)]

    def early_passes():
        slots = [ring(1), ring(3), ring(2), across]
        return [current_copy(x, partner, cg_pass.at[k]) for k, x in enumerate(slots)]

    def late_passes():
        slots = [ring_across(1), ring_across(3), ring_across(2)]
        return [current_copy(x, partner, cg_pass.at[4 + k]) for k, x in enumerate(slots)]

    inv_copy.wait()
    src_copy.wait()
    b0h, b0l = split(inv[0])
    b1h, b1l = split(inv[1])
    put_embedded(vhi, 0, b0h, b1h)
    put_embedded(vlo, 0, b0l, b1l)

    def apply_inverse(x):
        xh, xl = split(x)
        return dot(xh, vhi[...]) + dot(xl, vhi[...]) + dot(xh, vlo[...])

    def source():
        re, im = field(src, slice(None), 0, 16)
        return jnp.concatenate([re.reshape(192, 128), im.reshape(192, 128)], axis=1)

    def publish(ref, at_, x):
        rows, start = at_
        ref[rows, pl.ds(start, 16, stride=2), :] = x[:, :128].reshape(12, 16, 128)
        ref[rows, pl.ds(start + 1, 16, stride=2), :] = x[:, 128:].reshape(12, 16, 128)

    adj[...] = apply_inverse(source())
    publish(ext.at[0], (slice(3, 15), 8), adj[...])
    own_current.wait()
    pl.semaphore_wait(barrier, greetings)

    def middle_first(t):
        return jnp.where(t == 0, 3, jnp.where(t < 4, t - 1, t))

    def sweep(s, carry):
        for d in range(len(DIRS)):
            halo_copy(s, d).start()
        @pl.when(s == 0)
        def _():
            for copy in own_sends():
                copy.start()

            def prepare(a, carry):
                lag_copy(a).wait()

                def one(b, carry):
                    h0, l0 = split(stage[a, b, 0])
                    h1, l1 = split(stage[a, b, 1])
                    base = pl.multiple_of(b * 256, 256)
                    put_embedded(whi.at[a], base, h0, h1)
                    put_embedded(wlo.at[a], base, l0, l1)
                    return carry

                return lax.fori_loop(0, 7, one, carry)

            lax.fori_loop(0, 7, prepare, 0)

        @pl.when(s > 0)
        def _():
            for copy in early_passes():
                copy.wait_recv()
                copy.start()
            for copy in relays():
                copy.start()

        def close_sides(rows, count):
            @pl.when(c == 0)
            def _():
                ext[s, rows, 0:8, :] = jnp.zeros((count, 8, 128), F32)

            @pl.when(c == n - 1)
            def _():
                ext[s, rows, 40:48, :] = jnp.zeros((count, 8, 128), F32)

        def build(rows):
            for b in range(7):
                for h in range(2):
                    hi, lo = split(ext[s, rows, pl.ds(2 * (b + 1) + h, 16, stride=2), :])
                    lanes = slice(b * 256 + h * 128, b * 256 + h * 128 + 128)
                    near_hi[rows, :, lanes] = hi
                    near_lo[rows, :, lanes] = lo

        for d in SIDES:
            halo_copy(s, d).wait_recv()
        close_sides(slice(3, 15), 12)
        build(slice(3, 15))
        total[...] = jnp.zeros_like(total)

        def lag_row(t, carry):
            a = middle_first(t)

            @pl.when(t == 1)
            def _():
                for d in REST:
                    halo_copy(s, d).wait_recv()

                @pl.when(r == 0)
                def _():
                    ext[s, 0:3] = jnp.zeros((3, 48, 128), F32)

                @pl.when(r == n - 1)
                def _():
                    ext[s, 15:18] = jnp.zeros((3, 48, 128), F32)

                close_sides(slice(0, 3), 3)
                close_sides(slice(15, 18), 3)
                build(slice(0, 3))
                build(slice(15, 18))

            hi = near_hi[pl.ds(a, 12)].reshape(192, 1792)
            lo = near_lo[pl.ds(a, 12)].reshape(192, 1792)
            total[...] += dot(hi, whi[a]) + dot(lo, whi[a]) + dot(hi, wlo[a])
            return carry

        lax.fori_loop(0, 7, lag_row, 0)
        adj[...] += apply_inverse(source() - adj[...] - total[...])
        @pl.when(s + 1 < SWEEPS)
        def _():
            publish(ext.at[lax.rem(s + 1, SWEEPS)], (slice(3, 15), 8), adj[...])

        return carry

    lax.fori_loop(0, SWEEPS, sweep, 0)

    for h in range(2):
        part = adj[:, h * 128:h * 128 + 128]
        part = jnp.concatenate([part, jnp.zeros((64, 128), F32)], axis=0)
        at[h] = part.T.reshape(16, 8, 256)

    def slice_copy(k, slot):
        return pltpu.make_async_remote_copy(
            src_ref=at.at[:, wrap(c + k)], dst_ref=ra.at[slot],
            send_sem=ra_send.at[k], recv_sem=ra_recv.at[k],
            device_id=(r, wrap(c + k)), device_id_type=MESH,
        )

    each(1, lambda k: slice_copy(k, c).start())
    own_slice = pltpu.make_async_copy(at.at[:, c], ra.at[c], own_sem.at[1])
    own_slice.start()
    publish(out, (slice(None), 0), adj[...])

    for copy in late_passes():
        copy.wait_recv()
        copy.start()

    def convert(t):
        base = pl.multiple_of(t * 16, 16)
        for h in range(2):
            hi, lo = split(cg[t, :, pl.ds(h, 16, stride=2), :])
            chi[:, pl.ds(base, 16), h * 128:h * 128 + 128] = hi
            clo[:, pl.ds(base, 16), h * 128:h * 128 + 128] = lo

    for dx in range(4):
        other = ring(dx) + 1 - 2 * core
        current_copy(other, partner, cg_send.at[4]).wait_recv()
        current_copy(lax.rem(other + 8, n), partner, cg_send.at[4]).wait_recv()
    lax.fori_loop(0, n, lambda t, carry: (convert(t), carry)[1], 0)

    own_slice.wait()
    each(1, lambda k: slice_copy(k, wrap(c - k)).wait_recv())

    lane = lax.broadcasted_iota(jnp.int32, (16, 128), 1) // 16
    for i in range(12):
        block = slice((i // 8) * 128, (i // 8) * 128 + 128)
        for half in range(2):
            row = jnp.zeros((16, 128), F32)
            for t in range(8):
                x = ra[half * 8 + t, :, :, block].reshape(16, 128)
                shift = ((t - i % 8) * 16) % 128
                if shift:
                    x = pltpu.roll(x, shift, 1)
                row = jnp.where(lane == t, x, row)
            strip[3 + i, :, half * 128:half * 128 + 128] = row

    def edge_copy(d):
        src_, dst, to = ((3, 15, wrap(r - 1)), (12, 0, wrap(r + 1)))[d]
        return pltpu.make_async_remote_copy(
            src_ref=strip.at[pl.ds(src_, 3)], dst_ref=strip.at[pl.ds(dst, 3)],
            send_sem=halo_send.at[d], recv_sem=halo_recv.at[d],
            device_id=(to, c), device_id_type=MESH,
        )

    for d in range(2):
        edge_copy(d).start()

    column = lax.broadcasted_iota(jnp.int32, (16, 256), 1)

    def spread(e, carry):
        x = strip[e]
        for b in range(7):
            y = x if b == 3 else pltpu.roll(x, (3 - b) % 256, 1)
            if b < 3:
                y = jnp.where(column >= 3 - b, y, 0.0)
            if b > 3:
                y = jnp.where(column < 256 - (b - 3), y, 0.0)
            hi, lo = split(y)
            a7h[e, b * 16:b * 16 + 16, :] = hi
            a7l[e, b * 16:b * 16 + 16, :] = lo
        return carry

    lax.fori_loop(3, 15, spread, 0)

    def reduce_copy(p, slot):
        return pltpu.make_async_remote_copy(
            src_ref=terms.at[p], dst_ref=gathered.at[slot],
            send_sem=red_send.at[p], recv_sem=red_recv.at[slot],
            device_id=(p, c), device_id_type=MESH,
        )

    def keep_copy():
        return pltpu.make_async_copy(terms.at[r], gathered.at[r], own_sem.at[2])

    def correlate(t, carry):
        a = middle_first(t)

        @pl.when(t == 1)
        def _():
            for d in range(2):
                edge_copy(d).wait_recv()

            @pl.when(r == 0)
            def _():
                strip[0:3] = jnp.zeros((3, 16, 256), F32)

            @pl.when(r == n - 1)
            def _():
                strip[15:18] = jnp.zeros((3, 16, 256), F32)

            lax.fori_loop(0, 3, spread, 0)
            lax.fori_loop(15, 18, spread, 0)

        high = jnp.concatenate([a7h[a + i] for i in range(12)], axis=1)
        low = jnp.concatenate([a7l[a + i] for i in range(12)], axis=1)
        both = dot(jnp.concatenate([high, low], axis=0), chi[...].reshape(3072, 256))
        rest = dot(high, clo[...].reshape(3072, 256))
        x = (both[0:112] + both[112:224] + rest).reshape(7, 2, 8, 256)
        real = (x[:, 0, :, 0:128] + x[:, 1, :, 128:256]) * factor
        imag = (x[:, 1, :, 0:128] - x[:, 0, :, 128:256]) * factor
        for b in range(7):
            for h, part in ((0, real), (1, imag)):
                tile = b * 2 + h
                terms[a * 2 + tile // 7, tile % 7] = part[b]
        for e in range(2):
            p = a * 2 + e

            @pl.when(p != r)
            def _():
                reduce_copy(p, r).start()

            @pl.when(p == r)
            def _():
                keep_copy().start()

        return carry

    lax.fori_loop(0, 7, correlate, 0)

    @pl.when(r < 14)
    def _():
        def collect(k, carry):
            @pl.when(k == r)
            def _():
                keep_copy().wait()

            @pl.when(k != r)
            def _():
                reduce_copy(r, k).wait_recv()

            return carry

        lax.fori_loop(0, n, collect, 0)
        x = gathered[0]
        for k in range(1, n):
            x = x + gathered[k]
        piece[...] = x

    def swap_copy():
        return pltpu.make_async_remote_copy(
            src_ref=piece, dst_ref=swapped, send_sem=swap_send, recv_sem=swap_recv,
            device_id=(c, r), device_id_type=MESH,
        )

    @pl.when(jnp.logical_and(r != c, r < 14))
    def _():
        swap_copy().start()

    @pl.when(jnp.logical_and(r != c, c < 14))
    def _():
        swap_copy().wait_recv()

    @pl.when(jnp.logical_and(r == c, r < 14))
    def _():
        own = pltpu.make_async_copy(piece, swapped, own_sem.at[3])
        own.start()
        own.wait()

    @pl.when(jnp.logical_and(r != c, r < 14))
    def _():
        swap_copy().wait_send()

    def result_copy(k, slot):
        return pltpu.make_async_remote_copy(
            src_ref=swapped, dst_ref=result.at[slot],
            send_sem=res_send.at[k], recv_sem=res_recv.at[slot],
            device_id=(r, wrap(c + k)), device_id_type=MESH,
        )

    own_result = pltpu.make_async_copy(swapped, result.at[c], own_sem.at[4])

    @pl.when(c < 14)
    def _():
        each(1, lambda k: result_copy(k, c).start())
        own_result.start()

    def drain_reduce(p, carry):
        @pl.when(p != r)
        def _():
            reduce_copy(p, r).wait_send()

        return carry

    lax.fori_loop(0, 14, drain_reduce, 0)
    each(1, lambda k: slice_copy(k, c).wait_send())
    for copy in own_sends() + relays() + early_passes() + late_passes():
        copy.wait_send()
    for d in range(2):
        edge_copy(d).wait_send()
    for s in range(SWEEPS):
        for d in range(len(DIRS)):
            halo_copy(s, d).wait_send()

    def finish(p, carry):
        @pl.when(p == c)
        def _():
            own_result.wait()

        @pl.when(p != c)
        def _():
            result_copy(1, p).wait_recv()

        return carry

    lax.fori_loop(0, 14, finish, 0)
    grad[...] = result[0:14].reshape(98, 8, 128)

    @pl.when(c < 14)
    def _():
        each(1, lambda k: result_copy(k, c).wait_send())


def hand_out(adj, grad, adj_out, grad_out, adj_buf, grad_buf, sem):
    into = [
        pltpu.make_async_copy(adj, adj_buf, sem.at[0]),
        pltpu.make_async_copy(grad, grad_buf, sem.at[1]),
    ]
    back = [
        pltpu.make_async_copy(adj_buf, adj_out, sem.at[2]),
        pltpu.make_async_copy(grad_buf, grad_out, sem.at[3]),
    ]
    for copy in into:
        copy.start()
    for first, second in zip(into, back):
        first.wait()
        second.start()
    for copy in back:
        copy.wait()


def on_device(adjoint_source, saved_currents, lag_blocks, element_inverse):
    vmem = pl.BlockSpec(memory_space=pltpu.VMEM)
    hbm = pl.BlockSpec(memory_space=pl.ANY)
    dma = pltpu.SemaphoreType.DMA
    elements = 12 * lax.axis_size("row") * 16 * lax.axis_size("col")
    adjoint, lag_grad = pl.pallas_call(
        functools.partial(kernel, -1.0 / math.sqrt(elements)),
        out_shape=(
            jax.ShapeDtypeStruct((12, 32, 128), F32),
            jax.ShapeDtypeStruct((98, 8, 128), F32),
        ),
        in_specs=[pl.BlockSpec(memory_space=pltpu.HBM)] * 4,
        out_specs=(vmem, vmem),
        scratch_shapes=[
            pltpu.VMEM((12, 32, 128), F32),
            pltpu.VMEM((2, 128, 128), F32),
            pltpu.VMEM((7, 7, 2, 128, 128), F32),
            pltpu.VMEM((7, 1792, 256), BF16),
            pltpu.VMEM((7, 1792, 256), BF16),
            pltpu.VMEM((256, 256), BF16),
            pltpu.VMEM((256, 256), BF16),
            pltpu.VMEM((SWEEPS, 18, 48, 128), F32),
            pltpu.VMEM((18, 16, 1792), BF16),
            pltpu.VMEM((18, 16, 1792), BF16),
            pltpu.VMEM((192, 256), F32),
            pltpu.VMEM((192, 256), F32),
            pltpu.VMEM((16, 12, 32, 128), F32),
            pltpu.VMEM((12, 256, 256), BF16),
            pltpu.VMEM((12, 256, 256), BF16),
            pltpu.VMEM((2, 16, 8, 256), F32),
            pltpu.VMEM((16, 2, 8, 256), F32),
            pltpu.VMEM((18, 16, 256), F32),
            pltpu.VMEM((18, 112, 256), BF16),
            pltpu.VMEM((18, 112, 256), BF16),
            pltpu.VMEM((14, 7, 8, 128), F32),
            pltpu.VMEM((16, 7, 8, 128), F32),
            pltpu.VMEM((7, 8, 128), F32),
            pltpu.VMEM((7, 8, 128), F32),
            pltpu.VMEM((16, 7, 8, 128), F32),
            dma((7,)), dma((SWEEPS, 8)), dma((SWEEPS, 8)),
            dma((5,)), dma((4,)), dma((7,)), dma((16,)),
            dma((16,)), dma((16,)), dma((2,)), dma((2,)),
            dma((16,)), dma((16,)), dma(()), dma(()), dma((16,)), dma((16,)), dma((7,)),
        ],
        compiler_params=pltpu.CompilerParams(
            collective_id=0, has_side_effects=True, vmem_limit_bytes=62 * 1024 * 1024
        ),
        name="adjoint_gradient",
    )(
        adjoint_source.reshape(12, 32, 128),
        saved_currents.reshape(12, 32, 128),
        lag_blocks,
        element_inverse,
    )
    adjoint, lag_grad = pl.pallas_call(
        hand_out,
        out_shape=(
            jax.ShapeDtypeStruct((12, 32, 128), F32),
            jax.ShapeDtypeStruct((98, 8, 128), F32),
        ),
        in_specs=[hbm, hbm],
        out_specs=(hbm, hbm),
        scratch_shapes=[
            pltpu.VMEM((12, 32, 128), F32), pltpu.VMEM((98, 8, 128), F32), dma((4,)),
        ],
        compiler_params=pltpu.CompilerParams(vmem_limit_bytes=62 * 1024 * 1024),
        name="hand_out",
    )(adjoint, lag_grad)
    return (adjoint.reshape(12, 16, 2, 128), lag_grad.reshape(7, 7, 2, 8, 128))


def solution(mesh):
    return jax.shard_map(
        on_device,
        mesh=mesh,
        in_specs=(P("row", "col", None, None), P("row", "col", None, None), P(), P()),
        out_specs=(P("row", "col", None, None), P(None, None, None, "row", None)),
        check_vma=False,
    )
```

```python
import functools
import math

import jax
import jax.numpy as jnp
from jax import lax
from jax.experimental import pallas as pl
from jax.experimental.pallas import tpu as pltpu
from jax.sharding import PartitionSpec as P

SWEEPS = 2
F32 = jnp.float32
BF16 = jnp.bfloat16
MESH = pl.DeviceIdType.MESH
DIRS = ((-1, -1), (-1, 1), (1, -1), (1, 1), (0, -1), (0, 1), (-1, 0), (1, 0))
SIDES = (4, 5)
REST = (0, 1, 2, 3, 6, 7)


def split(x):
    hi = x.astype(BF16)
    lo = (x - hi.astype(F32)).astype(BF16)
    return hi, lo


def dot(x, y):
    return jnp.dot(x, y, preferred_element_type=F32)


def put_embedded(dst, base, a0, a1):
    dst[pl.ds(base, 128), 0:128] = a0
    dst[pl.ds(base, 128), 128:256] = -a1
    dst[pl.ds(base + 128, 128), 0:128] = a1
    dst[pl.ds(base + 128, 128), 128:256] = a0


def field(ref, rows, start, cols):
    re = ref[rows, pl.ds(start, cols, stride=2), :]
    im = ref[rows, pl.ds(start + 1, cols, stride=2), :]
    return re, im

def kernel(
    factor, src_hbm, cur, lag, inv_hbm, out, grad,
    src, inv, out_tile, stage, whi, wlo, vhi, vlo, ext, near_hi, near_lo, total, adj,
    cg, chi, clo, at, ra, strip, a7h, a7l, terms, gathered, piece, swapped, result,
    lag_sem, send_sem, recv_sem, cg_send, cg_relay, cg_pass, cg_recv,
    ra_send, ra_recv, halo_send, halo_recv, red_send, red_recv,
    swap_send, swap_recv, res_send, res_recv, own_sem, out_sem,
):
    n = 16
    r, c = lax.axis_index("row"), lax.axis_index("col")

    def wrap(x):
        return lax.rem(x + n, n)

    def each(first, body):
        def step(k, carry):
            body(k)
            return carry

        lax.fori_loop(first, n, step, 0)

    barrier = pltpu.get_barrier_semaphore()

    def greet(row, col):
        pl.semaphore_signal(barrier, inc=1, device_id=(row, col), device_id_type=MESH)

    each(1, lambda k: greet(r, wrap(c + k)))
    for dr in (-1, 1):
        for dc in (-1, 0, 1):
            greet(wrap(r + dr), wrap(c + dc))
    each(1, lambda k: greet(wrap(r + k), c))

    greetings = 15 + 6 + 15

    src_copy = pltpu.make_async_copy(src_hbm, src, own_sem.at[5])
    inv_copy = pltpu.make_async_copy(inv_hbm, inv, own_sem.at[6])
    src_copy.start()
    inv_copy.start()

    def lag_copy(a):
        return pltpu.make_async_copy(lag.at[a], stage.at[a], lag_sem.at[a])

    for a in range(7):
        lag_copy(a).start()
    own_current = pltpu.make_async_copy(cur, cg.at[c], own_sem.at[0])
    own_current.start()

    def box(dr, dc):
        rows = {-1: (3, 15, 3), 1: (12, 0, 3), 0: (3, 3, 12)}[dr]
        cols = {-1: (8, 40, 8), 1: (32, 0, 8), 0: (8, 8, 32)}[dc]
        return rows, cols

    def halo_copy(s, d):
        dr, dc = DIRS[d]
        (rs, rd, rn), (cs, cd, cn) = box(dr, dc)
        return pltpu.make_async_remote_copy(
            src_ref=ext.at[s, pl.ds(rs, rn), pl.ds(cs, cn), :],
            dst_ref=ext.at[s, pl.ds(rd, rn), pl.ds(cd, cn), :],
            send_sem=send_sem.at[s, d],
            recv_sem=recv_sem.at[s, d],
            device_id=(wrap(r + dr), wrap(c + dc)),
            device_id_type=MESH,
        )

    side, place, core = c // 8, lax.rem(c // 2, 4), lax.rem(c, 2)
    partner = c + 1 - 2 * core
    across = lax.rem(c + 8, n)

    def ring(dx):
        return side * 8 + lax.rem(place + dx, 4) * 2 + core

    def ring_across(dx):
        return lax.rem(ring(dx) + 8, n)

    def current_copy(slot, col, sem):
        return pltpu.make_async_remote_copy(
            src_ref=cg.at[slot], dst_ref=cg.at[slot],
            send_sem=sem, recv_sem=cg_recv.at[slot],
            device_id=(r, col), device_id_type=MESH,
        )

    def own_sends():
        return [current_copy(c, ring(dx), cg_send.at[dx]) for dx in (1, 3, 2)] + [
            current_copy(c, across, cg_send.at[0]),
            current_copy(c, partner, cg_send.at[4]),
        ]

    def relays():
        return [current_copy(across, ring(dx), cg_relay.at[dx]) for dx in (1, 3, 2)]

    def early_passes():
        slots = [ring(1), ring(3), ring(2), across]
        return [current_copy(x, partner, cg_pass.at[k]) for k, x in enumerate(slots)]

    def late_passes():
        slots = [ring_across(1), ring_across(3), ring_across(2)]
        return [current_copy(x, partner, cg_pass.at[4 + k]) for k, x in enumerate(slots)]

    inv_copy.wait()
    src_copy.wait()
    b0h, b0l = split(inv[0])
    b1h, b1l = split(inv[1])
    put_embedded(vhi, 0, b0h, b1h)
    put_embedded(vlo, 0, b0l, b1l)

    def apply_inverse(x):
        xh, xl = split(x)
        return dot(xh, vhi[...]) + dot(xl, vhi[...]) + dot(xh, vlo[...])

    def source():
        re, im = field(src, slice(None), 0, 16)
        return jnp.concatenate([re.reshape(192, 128), im.reshape(192, 128)], axis=1)

    def publish(ref, at_, x):
        rows, start = at_
        ref[rows, pl.ds(start, 16, stride=2), :] = x[:, :128].reshape(12, 16, 128)
        ref[rows, pl.ds(start + 1, 16, stride=2), :] = x[:, 128:].reshape(12, 16, 128)

    adj[...] = apply_inverse(source())
    publish(ext.at[0], (slice(3, 15), 8), adj[...])
    own_current.wait()
    pl.semaphore_wait(barrier, greetings)

    def middle_first(t):
        return jnp.where(t == 0, 3, jnp.where(t < 4, t - 1, t))

    def sweep(s, carry):
        for d in range(len(DIRS)):
            halo_copy(s, d).start()
        @pl.when(s == 0)
        def _():
            for copy in own_sends():
                copy.start()

            def prepare(a, carry):
                lag_copy(a).wait()

                def one(b, carry):
                    h0, l0 = split(stage[a, b, 0])
                    h1, l1 = split(stage[a, b, 1])
                    base = pl.multiple_of(b * 256, 256)
                    put_embedded(whi.at[a], base, h0, h1)
                    put_embedded(wlo.at[a], base, l0, l1)
                    return carry

                return lax.fori_loop(0, 7, one, carry)

            lax.fori_loop(0, 7, prepare, 0)

        @pl.when(s > 0)
        def _():
            for copy in early_passes():
                copy.wait_recv()
                copy.start()
            for copy in relays():
                copy.start()

        def close_sides(rows, count):
            @pl.when(c == 0)
            def _():
                ext[s, rows, 0:8, :] = jnp.zeros((count, 8, 128), F32)

            @pl.when(c == n - 1)
            def _():
                ext[s, rows, 40:48, :] = jnp.zeros((count, 8, 128), F32)

        def build(rows):
            for b in range(7):
                for h in range(2):
                    hi, lo = split(ext[s, rows, pl.ds(2 * (b + 1) + h, 16, stride=2), :])
                    lanes = slice(b * 256 + h * 128, b * 256 + h * 128 + 128)
                    near_hi[rows, :, lanes] = hi
                    near_lo[rows, :, lanes] = lo

        for d in SIDES:
            halo_copy(s, d).wait_recv()
        close_sides(slice(3, 15), 12)
        build(slice(3, 15))
        total[...] = jnp.zeros_like(total)

        def lag_row(t, carry):
            a = middle_first(t)

            @pl.when(t == 1)
            def _():
                for d in REST:
                    halo_copy(s, d).wait_recv()

                @pl.when(r == 0)
                def _():
                    ext[s, 0:3] = jnp.zeros((3, 48, 128), F32)

                @pl.when(r == n - 1)
                def _():
                    ext[s, 15:18] = jnp.zeros((3, 48, 128), F32)

                close_sides(slice(0, 3), 3)
                close_sides(slice(15, 18), 3)
                build(slice(0, 3))
                build(slice(15, 18))

            hi = near_hi[pl.ds(a, 12)].reshape(192, 1792)
            lo = near_lo[pl.ds(a, 12)].reshape(192, 1792)
            total[...] += dot(hi, whi[a]) + dot(lo, whi[a]) + dot(hi, wlo[a])
            return carry

        lax.fori_loop(0, 7, lag_row, 0)
        adj[...] += apply_inverse(source() - adj[...] - total[...])
        @pl.when(s + 1 < SWEEPS)
        def _():
            publish(ext.at[lax.rem(s + 1, SWEEPS)], (slice(3, 15), 8), adj[...])

        return carry

    lax.fori_loop(0, SWEEPS, sweep, 0)

    for h in range(2):
        part = adj[:, h * 128:h * 128 + 128]
        part = jnp.concatenate([part, jnp.zeros((64, 128), F32)], axis=0)
        at[h] = part.T.reshape(16, 8, 256)

    def slice_copy(k, slot):
        return pltpu.make_async_remote_copy(
            src_ref=at.at[:, wrap(c + k)], dst_ref=ra.at[slot],
            send_sem=ra_send.at[k], recv_sem=ra_recv.at[k],
            device_id=(r, wrap(c + k)), device_id_type=MESH,
        )

    each(1, lambda k: slice_copy(k, c).start())
    own_slice = pltpu.make_async_copy(at.at[:, c], ra.at[c], own_sem.at[1])
    own_slice.start()
    publish(out_tile, (slice(None), 0), adj[...])
    out_copy = pltpu.make_async_copy(out_tile, out, out_sem.at[14])
    out_copy.start()

    for copy in late_passes():
        copy.wait_recv()
        copy.start()

    def convert(t):
        base = pl.multiple_of(t * 16, 16)
        for h in range(2):
            hi, lo = split(cg[t, :, pl.ds(h, 16, stride=2), :])
            chi[:, pl.ds(base, 16), h * 128:h * 128 + 128] = hi
            clo[:, pl.ds(base, 16), h * 128:h * 128 + 128] = lo

    for dx in range(4):
        other = ring(dx) + 1 - 2 * core
        current_copy(other, partner, cg_send.at[4]).wait_recv()
        current_copy(lax.rem(other + 8, n), partner, cg_send.at[4]).wait_recv()
    lax.fori_loop(0, n, lambda t, carry: (convert(t), carry)[1], 0)

    own_slice.wait()
    each(1, lambda k: slice_copy(k, wrap(c - k)).wait_recv())

    lane = lax.broadcasted_iota(jnp.int32, (16, 128), 1) // 16
    for i in range(12):
        block = slice((i // 8) * 128, (i // 8) * 128 + 128)
        for half in range(2):
            row = jnp.zeros((16, 128), F32)
            for t in range(8):
                x = ra[half * 8 + t, :, :, block].reshape(16, 128)
                shift = ((t - i % 8) * 16) % 128
                if shift:
                    x = pltpu.roll(x, shift, 1)
                row = jnp.where(lane == t, x, row)
            strip[3 + i, :, half * 128:half * 128 + 128] = row

    def edge_copy(d):
        src_, dst, to = ((3, 15, wrap(r - 1)), (12, 0, wrap(r + 1)))[d]
        return pltpu.make_async_remote_copy(
            src_ref=strip.at[pl.ds(src_, 3)], dst_ref=strip.at[pl.ds(dst, 3)],
            send_sem=halo_send.at[d], recv_sem=halo_recv.at[d],
            device_id=(to, c), device_id_type=MESH,
        )

    for d in range(2):
        edge_copy(d).start()

    column = lax.broadcasted_iota(jnp.int32, (16, 256), 1)

    def spread(e, carry):
        x = strip[e]
        for b in range(7):
            y = x if b == 3 else pltpu.roll(x, (3 - b) % 256, 1)
            if b < 3:
                y = jnp.where(column >= 3 - b, y, 0.0)
            if b > 3:
                y = jnp.where(column < 256 - (b - 3), y, 0.0)
            hi, lo = split(y)
            a7h[e, b * 16:b * 16 + 16, :] = hi
            a7l[e, b * 16:b * 16 + 16, :] = lo
        return carry

    lax.fori_loop(3, 15, spread, 0)

    def reduce_copy(p, slot):
        return pltpu.make_async_remote_copy(
            src_ref=terms.at[p], dst_ref=gathered.at[slot],
            send_sem=red_send.at[p], recv_sem=red_recv.at[slot],
            device_id=(p, c), device_id_type=MESH,
        )

    def keep_copy():
        return pltpu.make_async_copy(terms.at[r], gathered.at[r], own_sem.at[2])

    def correlate(t, carry):
        a = middle_first(t)

        @pl.when(t == 1)
        def _():
            for d in range(2):
                edge_copy(d).wait_recv()

            @pl.when(r == 0)
            def _():
                strip[0:3] = jnp.zeros((3, 16, 256), F32)

            @pl.when(r == n - 1)
            def _():
                strip[15:18] = jnp.zeros((3, 16, 256), F32)

            lax.fori_loop(0, 3, spread, 0)
            lax.fori_loop(15, 18, spread, 0)

        high = jnp.concatenate([a7h[a + i] for i in range(12)], axis=1)
        low = jnp.concatenate([a7l[a + i] for i in range(12)], axis=1)
        both = dot(jnp.concatenate([high, low], axis=0), chi[...].reshape(3072, 256))
        rest = dot(high, clo[...].reshape(3072, 256))
        x = (both[0:112] + both[112:224] + rest).reshape(7, 2, 8, 256)
        real = (x[:, 0, :, 0:128] + x[:, 1, :, 128:256]) * factor
        imag = (x[:, 1, :, 0:128] - x[:, 0, :, 128:256]) * factor
        for b in range(7):
            for h, part in ((0, real), (1, imag)):
                tile = b * 2 + h
                terms[a * 2 + tile // 7, tile % 7] = part[b]
        for e in range(2):
            p = a * 2 + e

            @pl.when(p != r)
            def _():
                reduce_copy(p, r).start()

            @pl.when(p == r)
            def _():
                keep_copy().start()

        return carry

    lax.fori_loop(0, 7, correlate, 0)

    @pl.when(r < 14)
    def _():
        def collect(k, carry):
            @pl.when(k == r)
            def _():
                keep_copy().wait()

            @pl.when(k != r)
            def _():
                reduce_copy(r, k).wait_recv()

            return carry

        lax.fori_loop(0, n, collect, 0)
        x = gathered[0]
        for k in range(1, n):
            x = x + gathered[k]
        piece[...] = x

    def swap_copy():
        return pltpu.make_async_remote_copy(
            src_ref=piece, dst_ref=swapped, send_sem=swap_send, recv_sem=swap_recv,
            device_id=(c, r), device_id_type=MESH,
        )

    @pl.when(jnp.logical_and(r != c, r < 14))
    def _():
        swap_copy().start()

    @pl.when(jnp.logical_and(r != c, c < 14))
    def _():
        swap_copy().wait_recv()

    @pl.when(jnp.logical_and(r == c, r < 14))
    def _():
        own = pltpu.make_async_copy(piece, swapped, own_sem.at[3])
        own.start()
        own.wait()

    @pl.when(jnp.logical_and(r != c, r < 14))
    def _():
        swap_copy().wait_send()

    def result_copy(k, slot):
        return pltpu.make_async_remote_copy(
            src_ref=swapped, dst_ref=result.at[slot],
            send_sem=res_send.at[k], recv_sem=res_recv.at[slot],
            device_id=(r, wrap(c + k)), device_id_type=MESH,
        )

    own_result = pltpu.make_async_copy(swapped, result.at[c], own_sem.at[4])

    @pl.when(c < 14)
    def _():
        each(1, lambda k: result_copy(k, c).start())
        own_result.start()

    def drain_reduce(p, carry):
        @pl.when(p != r)
        def _():
            reduce_copy(p, r).wait_send()

        return carry

    lax.fori_loop(0, 14, drain_reduce, 0)
    each(1, lambda k: slice_copy(k, c).wait_send())
    for copy in own_sends() + relays() + early_passes() + late_passes():
        copy.wait_send()
    for d in range(2):
        edge_copy(d).wait_send()
    for s in range(SWEEPS):
        for d in range(len(DIRS)):
            halo_copy(s, d).wait_send()

    def grad_copy(p):
        return pltpu.make_async_copy(result.at[p], grad.at[pl.ds(p * 7, 7)], out_sem.at[p])

    def finish(p, carry):
        @pl.when(p == c)
        def _():
            own_result.wait()

        @pl.when(p != c)
        def _():
            result_copy(1, p).wait_recv()

        grad_copy(p).start()
        return carry

    lax.fori_loop(0, 14, finish, 0)
    out_copy.wait()
    lax.fori_loop(0, 14, lambda p, carry: (grad_copy(p).wait(), carry)[1], 0)

    @pl.when(c < 14)
    def _():
        each(1, lambda k: result_copy(k, c).wait_send())


def hand_out(adj, grad, adj_out, grad_out, adj_buf, grad_buf, sem):
    into = [
        pltpu.make_async_copy(adj, adj_buf, sem.at[0]),
        pltpu.make_async_copy(grad, grad_buf, sem.at[1]),
    ]
    back = [
        pltpu.make_async_copy(adj_buf, adj_out, sem.at[2]),
        pltpu.make_async_copy(grad_buf, grad_out, sem.at[3]),
    ]
    for copy in into:
        copy.start()
    for first, second in zip(into, back):
        first.wait()
        second.start()
    for copy in back:
        copy.wait()


def on_device(adjoint_source, saved_currents, lag_blocks, element_inverse):
    hbm = pl.BlockSpec(memory_space=pl.ANY)
    dma = pltpu.SemaphoreType.DMA
    elements = 12 * lax.axis_size("row") * 16 * lax.axis_size("col")
    adjoint, lag_grad = pl.pallas_call(
        functools.partial(kernel, -1.0 / math.sqrt(elements)),
        out_shape=(
            jax.ShapeDtypeStruct((12, 32, 128), F32),
            jax.ShapeDtypeStruct((98, 8, 128), F32),
        ),
        in_specs=[pl.BlockSpec(memory_space=pltpu.HBM)] * 4,
        out_specs=(pl.BlockSpec(memory_space=pltpu.HBM),) * 2,
        scratch_shapes=[
            pltpu.VMEM((12, 32, 128), F32),
            pltpu.VMEM((2, 128, 128), F32),
            pltpu.VMEM((12, 32, 128), F32),
            pltpu.VMEM((7, 7, 2, 128, 128), F32),
            pltpu.VMEM((7, 1792, 256), BF16),
            pltpu.VMEM((7, 1792, 256), BF16),
            pltpu.VMEM((256, 256), BF16),
            pltpu.VMEM((256, 256), BF16),
            pltpu.VMEM((SWEEPS, 18, 48, 128), F32),
            pltpu.VMEM((18, 16, 1792), BF16),
            pltpu.VMEM((18, 16, 1792), BF16),
            pltpu.VMEM((192, 256), F32),
            pltpu.VMEM((192, 256), F32),
            pltpu.VMEM((16, 12, 32, 128), F32),
            pltpu.VMEM((12, 256, 256), BF16),
            pltpu.VMEM((12, 256, 256), BF16),
            pltpu.VMEM((2, 16, 8, 256), F32),
            pltpu.VMEM((16, 2, 8, 256), F32),
            pltpu.VMEM((18, 16, 256), F32),
            pltpu.VMEM((18, 112, 256), BF16),
            pltpu.VMEM((18, 112, 256), BF16),
            pltpu.VMEM((14, 7, 8, 128), F32),
            pltpu.VMEM((16, 7, 8, 128), F32),
            pltpu.VMEM((7, 8, 128), F32),
            pltpu.VMEM((7, 8, 128), F32),
            pltpu.VMEM((16, 7, 8, 128), F32),
            dma((7,)), dma((SWEEPS, 8)), dma((SWEEPS, 8)),
            dma((5,)), dma((4,)), dma((7,)), dma((16,)),
            dma((16,)), dma((16,)), dma((2,)), dma((2,)),
            dma((16,)), dma((16,)), dma(()), dma(()), dma((16,)), dma((16,)), dma((7,)), dma((15,)),
        ],
        compiler_params=pltpu.CompilerParams(
            collective_id=0, has_side_effects=True, vmem_limit_bytes=62 * 1024 * 1024
        ),
        name="adjoint_gradient",
    )(
        adjoint_source.reshape(12, 32, 128),
        saved_currents.reshape(12, 32, 128),
        lag_blocks,
        element_inverse,
    )
    adjoint, lag_grad = pl.pallas_call(
        hand_out,
        out_shape=(
            jax.ShapeDtypeStruct((12, 32, 128), F32),
            jax.ShapeDtypeStruct((98, 8, 128), F32),
        ),
        in_specs=[hbm, hbm],
        out_specs=(hbm, hbm),
        scratch_shapes=[
            pltpu.VMEM((12, 32, 128), F32), pltpu.VMEM((98, 8, 128), F32), dma((4,)),
        ],
        compiler_params=pltpu.CompilerParams(vmem_limit_bytes=62 * 1024 * 1024),
        name="hand_out",
    )(adjoint, lag_grad)
    return (adjoint.reshape(12, 16, 2, 128), lag_grad.reshape(7, 7, 2, 8, 128))


def solution(mesh):
    return jax.shard_map(
        on_device,
        mesh=mesh,
        in_specs=(P("row", "col", None, None), P("row", "col", None, None), P(), P()),
        out_specs=(P("row", "col", None, None), P(None, None, None, "row", None)),
        check_vma=False,
    )
```

```python
import functools
import math

import jax
import jax.numpy as jnp
from jax import lax
from jax.experimental import pallas as pl
from jax.experimental.pallas import tpu as pltpu
from jax.sharding import PartitionSpec as P

SWEEPS = 2
F32 = jnp.float32
BF16 = jnp.bfloat16
MESH = pl.DeviceIdType.MESH
DIRS = ((-1, -1), (-1, 1), (1, -1), (1, 1), (0, -1), (0, 1), (-1, 0), (1, 0))
SIDES = (4, 5)
REST = (0, 1, 2, 3, 6, 7)


def split(x):
    hi = x.astype(BF16)
    lo = (x - hi.astype(F32)).astype(BF16)
    return hi, lo


def dot(x, y):
    return jnp.dot(x, y, preferred_element_type=F32)


def put_embedded(dst, base, a0, a1):
    dst[pl.ds(base, 128), 0:128] = a0
    dst[pl.ds(base, 128), 128:256] = -a1
    dst[pl.ds(base + 128, 128), 0:128] = a1
    dst[pl.ds(base + 128, 128), 128:256] = a0


def field(ref, rows, start, cols):
    re = ref[rows, pl.ds(start, cols, stride=2), :]
    im = ref[rows, pl.ds(start + 1, cols, stride=2), :]
    return re, im

def kernel(
    factor, src_hbm, cur, lag, inv_hbm, out, grad,
    src, inv, out_tile, stage, whi, wlo, vhi, vlo, ext, near_hi, near_lo, total, adj,
    cg, chi, clo, at, ra, strip, a7h, a7l, terms, gathered, piece, swapped, result,
    lag_sem, send_sem, recv_sem, cg_send, cg_relay, cg_pass, cg_recv,
    ra_send, ra_recv, halo_send, halo_recv, red_send, red_recv,
    swap_send, swap_recv, res_send, res_recv, own_sem, out_sem,
):
    n = 16
    r, c = lax.axis_index("row"), lax.axis_index("col")

    def wrap(x):
        return lax.rem(x + n, n)

    def each(first, body):
        def step(k, carry):
            body(k)
            return carry

        lax.fori_loop(first, n, step, 0)

    barrier = pltpu.get_barrier_semaphore()

    def greet(row, col):
        pl.semaphore_signal(barrier, inc=1, device_id=(row, col), device_id_type=MESH)

    each(1, lambda k: greet(r, wrap(c + k)))
    for dr in (-1, 1):
        for dc in (-1, 0, 1):
            greet(wrap(r + dr), wrap(c + dc))
    each(1, lambda k: greet(wrap(r + k), c))

    greetings = 15 + 6 + 15

    src_copy = pltpu.make_async_copy(src_hbm, src, own_sem.at[5])
    inv_copy = pltpu.make_async_copy(inv_hbm, inv, own_sem.at[6])
    src_copy.start()
    inv_copy.start()

    def lag_copy(a):
        return pltpu.make_async_copy(lag.at[a], stage.at[a], lag_sem.at[a])

    for a in range(7):
        lag_copy(a).start()
    own_current = pltpu.make_async_copy(cur, cg.at[c], own_sem.at[0])
    own_current.start()

    def box(dr, dc):
        rows = {-1: (3, 15, 3), 1: (12, 0, 3), 0: (3, 3, 12)}[dr]
        cols = {-1: (8, 40, 8), 1: (32, 0, 8), 0: (8, 8, 32)}[dc]
        return rows, cols

    def halo_copy(s, d):
        dr, dc = DIRS[d]
        (rs, rd, rn), (cs, cd, cn) = box(dr, dc)
        return pltpu.make_async_remote_copy(
            src_ref=ext.at[s, pl.ds(rs, rn), pl.ds(cs, cn), :],
            dst_ref=ext.at[s, pl.ds(rd, rn), pl.ds(cd, cn), :],
            send_sem=send_sem.at[s, d],
            recv_sem=recv_sem.at[s, d],
            device_id=(wrap(r + dr), wrap(c + dc)),
            device_id_type=MESH,
        )

    side, place, core = c // 8, lax.rem(c // 2, 4), lax.rem(c, 2)
    partner = c + 1 - 2 * core
    across = lax.rem(c + 8, n)

    def ring(dx):
        return side * 8 + lax.rem(place + dx, 4) * 2 + core

    def ring_across(dx):
        return lax.rem(ring(dx) + 8, n)

    def current_copy(slot, col, sem):
        return pltpu.make_async_remote_copy(
            src_ref=cg.at[slot], dst_ref=cg.at[slot],
            send_sem=sem, recv_sem=cg_recv.at[slot],
            device_id=(r, col), device_id_type=MESH,
        )

    def own_sends():
        return [current_copy(c, ring(dx), cg_send.at[dx]) for dx in (1, 3, 2)] + [
            current_copy(c, across, cg_send.at[0]),
            current_copy(c, partner, cg_send.at[4]),
        ]

    def relays():
        return [current_copy(across, ring(dx), cg_relay.at[dx]) for dx in (1, 3, 2)]

    def early_passes():
        slots = [ring(1), ring(3), ring(2), across]
        return [current_copy(x, partner, cg_pass.at[k]) for k, x in enumerate(slots)]

    def late_passes():
        slots = [ring_across(1), ring_across(3), ring_across(2)]
        return [current_copy(x, partner, cg_pass.at[4 + k]) for k, x in enumerate(slots)]

    inv_copy.wait()
    src_copy.wait()
    b0h, b0l = split(inv[0])
    b1h, b1l = split(inv[1])
    put_embedded(vhi, 0, b0h, b1h)
    put_embedded(vlo, 0, b0l, b1l)

    def apply_inverse(x):
        xh, xl = split(x)
        return dot(xh, vhi[...]) + dot(xl, vhi[...]) + dot(xh, vlo[...])

    def source():
        re, im = field(src, slice(None), 0, 16)
        return jnp.concatenate([re.reshape(192, 128), im.reshape(192, 128)], axis=1)

    def publish(ref, at_, x):
        rows, start = at_
        ref[rows, pl.ds(start, 16, stride=2), :] = x[:, :128].reshape(12, 16, 128)
        ref[rows, pl.ds(start + 1, 16, stride=2), :] = x[:, 128:].reshape(12, 16, 128)

    adj[...] = apply_inverse(source())
    publish(ext.at[0], (slice(3, 15), 8), adj[...])
    own_current.wait()
    pl.semaphore_wait(barrier, greetings)

    def middle_first(t):
        return jnp.where(t == 0, 3, jnp.where(t < 4, t - 1, t))

    def sweep(s, carry):
        for d in range(len(DIRS)):
            halo_copy(s, d).start()
        @pl.when(s == 0)
        def _():
            for copy in own_sends():
                copy.start()

            def prepare(a, carry):
                lag_copy(a).wait()

                def one(b, carry):
                    h0, l0 = split(stage[a, b, 0])
                    h1, l1 = split(stage[a, b, 1])
                    base = pl.multiple_of(b * 256, 256)
                    put_embedded(whi.at[a], base, h0, h1)
                    put_embedded(wlo.at[a], base, l0, l1)
                    return carry

                return lax.fori_loop(0, 7, one, carry)

            lax.fori_loop(0, 7, prepare, 0)

        @pl.when(s > 0)
        def _():
            for copy in early_passes():
                copy.wait_recv()
                copy.start()
            for copy in relays():
                copy.start()

        def close_sides(rows, count):
            @pl.when(c == 0)
            def _():
                ext[s, rows, 0:8, :] = jnp.zeros((count, 8, 128), F32)

            @pl.when(c == n - 1)
            def _():
                ext[s, rows, 40:48, :] = jnp.zeros((count, 8, 128), F32)

        def build(rows):
            for b in range(7):
                for h in range(2):
                    hi, lo = split(ext[s, rows, pl.ds(2 * (b + 1) + h, 16, stride=2), :])
                    lanes = slice(b * 256 + h * 128, b * 256 + h * 128 + 128)
                    near_hi[rows, :, lanes] = hi
                    near_lo[rows, :, lanes] = lo

        for d in SIDES:
            halo_copy(s, d).wait_recv()
        close_sides(slice(3, 15), 12)
        build(slice(3, 15))
        total[...] = jnp.zeros_like(total)

        def lag_row(t, carry):
            a = middle_first(t)

            @pl.when(t == 1)
            def _():
                for d in REST:
                    halo_copy(s, d).wait_recv()

                @pl.when(r == 0)
                def _():
                    ext[s, 0:3] = jnp.zeros((3, 48, 128), F32)

                @pl.when(r == n - 1)
                def _():
                    ext[s, 15:18] = jnp.zeros((3, 48, 128), F32)

                close_sides(slice(0, 3), 3)
                close_sides(slice(15, 18), 3)
                build(slice(0, 3))
                build(slice(15, 18))

            hi = near_hi[pl.ds(a, 12)].reshape(192, 1792)
            lo = near_lo[pl.ds(a, 12)].reshape(192, 1792)
            total[...] += dot(hi, whi[a]) + dot(lo, whi[a]) + dot(hi, wlo[a])
            return carry

        lax.fori_loop(0, 7, lag_row, 0)
        adj[...] += apply_inverse(source() - adj[...] - total[...])
        @pl.when(s + 1 < SWEEPS)
        def _():
            publish(ext.at[lax.rem(s + 1, SWEEPS)], (slice(3, 15), 8), adj[...])

        return carry

    lax.fori_loop(0, SWEEPS, sweep, 0)

    for h in range(2):
        part = adj[:, h * 128:h * 128 + 128]
        part = jnp.concatenate([part, jnp.zeros((64, 128), F32)], axis=0)
        at[h] = part.T.reshape(16, 8, 256)

    def slice_copy(k, slot):
        return pltpu.make_async_remote_copy(
            src_ref=at.at[:, wrap(c + k)], dst_ref=ra.at[slot],
            send_sem=ra_send.at[k], recv_sem=ra_recv.at[k],
            device_id=(r, wrap(c + k)), device_id_type=MESH,
        )

    each(1, lambda k: slice_copy(k, c).start())
    own_slice = pltpu.make_async_copy(at.at[:, c], ra.at[c], own_sem.at[1])
    own_slice.start()
    publish(out_tile, (slice(None), 0), adj[...])
    out_copy = pltpu.make_async_copy(out_tile, out, out_sem.at[14])
    out_copy.start()

    for copy in late_passes():
        copy.wait_recv()
        copy.start()

    def convert(t):
        base = pl.multiple_of(t * 16, 16)
        for h in range(2):
            hi, lo = split(cg[t, :, pl.ds(h, 16, stride=2), :])
            chi[:, pl.ds(base, 16), h * 128:h * 128 + 128] = hi
            clo[:, pl.ds(base, 16), h * 128:h * 128 + 128] = lo

    for dx in range(4):
        other = ring(dx) + 1 - 2 * core
        current_copy(other, partner, cg_send.at[4]).wait_recv()
        current_copy(lax.rem(other + 8, n), partner, cg_send.at[4]).wait_recv()
    lax.fori_loop(0, n, lambda t, carry: (convert(t), carry)[1], 0)

    own_slice.wait()
    each(1, lambda k: slice_copy(k, wrap(c - k)).wait_recv())

    lane = lax.broadcasted_iota(jnp.int32, (16, 128), 1) // 16
    for i in range(12):
        block = slice((i // 8) * 128, (i // 8) * 128 + 128)
        for half in range(2):
            row = jnp.zeros((16, 128), F32)
            for t in range(8):
                x = ra[half * 8 + t, :, :, block].reshape(16, 128)
                shift = ((t - i % 8) * 16) % 128
                if shift:
                    x = pltpu.roll(x, shift, 1)
                row = jnp.where(lane == t, x, row)
            strip[3 + i, :, half * 128:half * 128 + 128] = row

    def edge_copy(d):
        src_, dst, to = ((3, 15, wrap(r - 1)), (12, 0, wrap(r + 1)))[d]
        return pltpu.make_async_remote_copy(
            src_ref=strip.at[pl.ds(src_, 3)], dst_ref=strip.at[pl.ds(dst, 3)],
            send_sem=halo_send.at[d], recv_sem=halo_recv.at[d],
            device_id=(to, c), device_id_type=MESH,
        )

    for d in range(2):
        edge_copy(d).start()

    column = lax.broadcasted_iota(jnp.int32, (16, 256), 1)

    def spread(e, carry):
        x = strip[e]
        for b in range(7):
            y = x if b == 3 else pltpu.roll(x, (3 - b) % 256, 1)
            if b < 3:
                y = jnp.where(column >= 3 - b, y, 0.0)
            if b > 3:
                y = jnp.where(column < 256 - (b - 3), y, 0.0)
            hi, lo = split(y)
            a7h[e, b * 16:b * 16 + 16, :] = hi
            a7l[e, b * 16:b * 16 + 16, :] = lo
        return carry

    lax.fori_loop(3, 15, spread, 0)

    def reduce_copy(p, slot):
        return pltpu.make_async_remote_copy(
            src_ref=terms.at[p], dst_ref=gathered.at[slot],
            send_sem=red_send.at[p], recv_sem=red_recv.at[slot],
            device_id=(p, c), device_id_type=MESH,
        )

    def keep_copy():
        return pltpu.make_async_copy(terms.at[r], gathered.at[r], own_sem.at[2])

    def correlate(t, carry):
        other = lax.rem(r // 2 + t, 6)
        a = jnp.where(t == 0, 3, other + jnp.where(other >= 3, 1, 0))

        @pl.when(t == 1)
        def _():
            for d in range(2):
                edge_copy(d).wait_recv()

            @pl.when(r == 0)
            def _():
                strip[0:3] = jnp.zeros((3, 16, 256), F32)

            @pl.when(r == n - 1)
            def _():
                strip[15:18] = jnp.zeros((3, 16, 256), F32)

            lax.fori_loop(0, 3, spread, 0)
            lax.fori_loop(15, 18, spread, 0)

        high = jnp.concatenate([a7h[a + i] for i in range(12)], axis=1)
        low = jnp.concatenate([a7l[a + i] for i in range(12)], axis=1)
        both = dot(jnp.concatenate([high, low], axis=0), chi[...].reshape(3072, 256))
        rest = dot(high, clo[...].reshape(3072, 256))
        x = (both[0:112] + both[112:224] + rest).reshape(7, 2, 8, 256)
        real = (x[:, 0, :, 0:128] + x[:, 1, :, 128:256]) * factor
        imag = (x[:, 1, :, 0:128] - x[:, 0, :, 128:256]) * factor
        for b in range(7):
            for h, part in ((0, real), (1, imag)):
                tile = b * 2 + h
                terms[a * 2 + tile // 7, tile % 7] = part[b]
        for e in range(2):
            p = a * 2 + e

            @pl.when(p != r)
            def _():
                reduce_copy(p, r).start()

            @pl.when(p == r)
            def _():
                keep_copy().start()

        return carry

    lax.fori_loop(0, 7, correlate, 0)

    @pl.when(r < 14)
    def _():
        def collect(k, carry):
            @pl.when(k == r)
            def _():
                keep_copy().wait()

            @pl.when(k != r)
            def _():
                reduce_copy(r, k).wait_recv()

            return carry

        lax.fori_loop(0, n, collect, 0)
        x = gathered[0]
        for k in range(1, n):
            x = x + gathered[k]
        piece[...] = x

    def swap_copy():
        return pltpu.make_async_remote_copy(
            src_ref=piece, dst_ref=swapped, send_sem=swap_send, recv_sem=swap_recv,
            device_id=(c, r), device_id_type=MESH,
        )

    @pl.when(jnp.logical_and(r != c, r < 14))
    def _():
        swap_copy().start()

    @pl.when(jnp.logical_and(r != c, c < 14))
    def _():
        swap_copy().wait_recv()

    @pl.when(jnp.logical_and(r == c, r < 14))
    def _():
        own = pltpu.make_async_copy(piece, swapped, own_sem.at[3])
        own.start()
        own.wait()

    @pl.when(jnp.logical_and(r != c, r < 14))
    def _():
        swap_copy().wait_send()

    def result_copy(k, slot):
        return pltpu.make_async_remote_copy(
            src_ref=swapped, dst_ref=result.at[slot],
            send_sem=res_send.at[k], recv_sem=res_recv.at[slot],
            device_id=(r, wrap(c + k)), device_id_type=MESH,
        )

    own_result = pltpu.make_async_copy(swapped, result.at[c], own_sem.at[4])

    @pl.when(c < 14)
    def _():
        each(1, lambda k: result_copy(k, c).start())
        own_result.start()

    def drain_reduce(p, carry):
        @pl.when(p != r)
        def _():
            reduce_copy(p, r).wait_send()

        return carry

    lax.fori_loop(0, 14, drain_reduce, 0)
    each(1, lambda k: slice_copy(k, c).wait_send())
    for copy in own_sends() + relays() + early_passes() + late_passes():
        copy.wait_send()
    for d in range(2):
        edge_copy(d).wait_send()
    for s in range(SWEEPS):
        for d in range(len(DIRS)):
            halo_copy(s, d).wait_send()

    def grad_copy(p):
        return pltpu.make_async_copy(result.at[p], grad.at[pl.ds(p * 7, 7)], out_sem.at[p])

    def finish(p, carry):
        @pl.when(p == c)
        def _():
            own_result.wait()

        @pl.when(p != c)
        def _():
            result_copy(1, p).wait_recv()

        grad_copy(p).start()
        return carry

    lax.fori_loop(0, 14, finish, 0)
    out_copy.wait()
    lax.fori_loop(0, 14, lambda p, carry: (grad_copy(p).wait(), carry)[1], 0)

    @pl.when(c < 14)
    def _():
        each(1, lambda k: result_copy(k, c).wait_send())


def hand_out(adj, grad, adj_out, grad_out, adj_buf, grad_buf, sem):
    into = [
        pltpu.make_async_copy(adj, adj_buf, sem.at[0]),
        pltpu.make_async_copy(grad, grad_buf, sem.at[1]),
    ]
    back = [
        pltpu.make_async_copy(adj_buf, adj_out, sem.at[2]),
        pltpu.make_async_copy(grad_buf, grad_out, sem.at[3]),
    ]
    for copy in into:
        copy.start()
    for first, second in zip(into, back):
        first.wait()
        second.start()
    for copy in back:
        copy.wait()


def on_device(adjoint_source, saved_currents, lag_blocks, element_inverse):
    hbm = pl.BlockSpec(memory_space=pl.ANY)
    dma = pltpu.SemaphoreType.DMA
    elements = 12 * lax.axis_size("row") * 16 * lax.axis_size("col")
    adjoint, lag_grad = pl.pallas_call(
        functools.partial(kernel, -1.0 / math.sqrt(elements)),
        out_shape=(
            jax.ShapeDtypeStruct((12, 32, 128), F32),
            jax.ShapeDtypeStruct((98, 8, 128), F32),
        ),
        in_specs=[pl.BlockSpec(memory_space=pltpu.HBM)] * 4,
        out_specs=(pl.BlockSpec(memory_space=pltpu.HBM),) * 2,
        scratch_shapes=[
            pltpu.VMEM((12, 32, 128), F32),
            pltpu.VMEM((2, 128, 128), F32),
            pltpu.VMEM((12, 32, 128), F32),
            pltpu.VMEM((7, 7, 2, 128, 128), F32),
            pltpu.VMEM((7, 1792, 256), BF16),
            pltpu.VMEM((7, 1792, 256), BF16),
            pltpu.VMEM((256, 256), BF16),
            pltpu.VMEM((256, 256), BF16),
            pltpu.VMEM((SWEEPS, 18, 48, 128), F32),
            pltpu.VMEM((18, 16, 1792), BF16),
            pltpu.VMEM((18, 16, 1792), BF16),
            pltpu.VMEM((192, 256), F32),
            pltpu.VMEM((192, 256), F32),
            pltpu.VMEM((16, 12, 32, 128), F32),
            pltpu.VMEM((12, 256, 256), BF16),
            pltpu.VMEM((12, 256, 256), BF16),
            pltpu.VMEM((2, 16, 8, 256), F32),
            pltpu.VMEM((16, 2, 8, 256), F32),
            pltpu.VMEM((18, 16, 256), F32),
            pltpu.VMEM((18, 112, 256), BF16),
            pltpu.VMEM((18, 112, 256), BF16),
            pltpu.VMEM((14, 7, 8, 128), F32),
            pltpu.VMEM((16, 7, 8, 128), F32),
            pltpu.VMEM((7, 8, 128), F32),
            pltpu.VMEM((7, 8, 128), F32),
            pltpu.VMEM((16, 7, 8, 128), F32),
            dma((7,)), dma((SWEEPS, 8)), dma((SWEEPS, 8)),
            dma((5,)), dma((4,)), dma((7,)), dma((16,)),
            dma((16,)), dma((16,)), dma((2,)), dma((2,)),
            dma((16,)), dma((16,)), dma(()), dma(()), dma((16,)), dma((16,)), dma((7,)), dma((15,)),
        ],
        compiler_params=pltpu.CompilerParams(
            collective_id=0, has_side_effects=True, vmem_limit_bytes=62 * 1024 * 1024
        ),
        name="adjoint_gradient",
    )(
        adjoint_source.reshape(12, 32, 128),
        saved_currents.reshape(12, 32, 128),
        lag_blocks,
        element_inverse,
    )
    adjoint, lag_grad = pl.pallas_call(
        hand_out,
        out_shape=(
            jax.ShapeDtypeStruct((12, 32, 128), F32),
            jax.ShapeDtypeStruct((98, 8, 128), F32),
        ),
        in_specs=[hbm, hbm],
        out_specs=(hbm, hbm),
        scratch_shapes=[
            pltpu.VMEM((12, 32, 128), F32), pltpu.VMEM((98, 8, 128), F32), dma((4,)),
        ],
        compiler_params=pltpu.CompilerParams(vmem_limit_bytes=62 * 1024 * 1024),
        name="hand_out",
    )(adjoint, lag_grad)
    return (adjoint.reshape(12, 16, 2, 128), lag_grad.reshape(7, 7, 2, 8, 128))


def solution(mesh):
    return jax.shard_map(
        on_device,
        mesh=mesh,
        in_specs=(P("row", "col", None, None), P("row", "col", None, None), P(), P()),
        out_specs=(P("row", "col", None, None), P(None, None, None, "row", None)),
        check_vma=False,
    )
```

```python
import functools
import math

import jax
import jax.numpy as jnp
from jax import lax
from jax.experimental import pallas as pl
from jax.experimental.pallas import tpu as pltpu
from jax.sharding import PartitionSpec as P

SWEEPS = 2
F32 = jnp.float32
BF16 = jnp.bfloat16
MESH = pl.DeviceIdType.MESH
DIRS = ((-1, -1), (-1, 1), (1, -1), (1, 1), (0, -1), (0, 1), (-1, 0), (1, 0))
SIDES = (4, 5)
REST = (0, 1, 2, 3, 6, 7)


def split(x):
    hi = x.astype(BF16)
    lo = (x - hi.astype(F32)).astype(BF16)
    return hi, lo


def dot(x, y):
    return jnp.dot(x, y, preferred_element_type=F32)


def put_embedded(dst, base, a0, a1):
    dst[pl.ds(base, 128), 0:128] = a0
    dst[pl.ds(base, 128), 128:256] = -a1
    dst[pl.ds(base + 128, 128), 0:128] = a1
    dst[pl.ds(base + 128, 128), 128:256] = a0


def field(ref, rows, start, cols):
    re = ref[rows, pl.ds(start, cols, stride=2), :]
    im = ref[rows, pl.ds(start + 1, cols, stride=2), :]
    return re, im

def kernel(
    factor, src_hbm, cur, lag, inv_hbm, out, grad,
    src, inv, out_tile, stage, whi, wlo, vhi, vlo, ext, near_hi, near_lo, total, adj,
    cg, chi, clo, at, ra, strip, a7h, a7l, terms, gathered, piece, swapped, result,
    lag_sem, send_sem, recv_sem, cg_send, cg_relay, cg_pass, cg_recv,
    ra_send, ra_recv, halo_send, halo_recv, red_send, red_recv,
    swap_send, swap_recv, res_send, res_recv, own_sem, out_sem,
):
    n = 16
    r, c = lax.axis_index("row"), lax.axis_index("col")

    def wrap(x):
        return lax.rem(x + n, n)

    def each(first, body):
        def step(k, carry):
            body(k)
            return carry

        lax.fori_loop(first, n, step, 0)

    barrier = pltpu.get_barrier_semaphore()

    def greet(row, col):
        pl.semaphore_signal(barrier, inc=1, device_id=(row, col), device_id_type=MESH)

    each(1, lambda k: greet(r, wrap(c + k)))
    for dr in (-1, 1):
        for dc in (-1, 0, 1):
            greet(wrap(r + dr), wrap(c + dc))
    each(1, lambda k: greet(wrap(r + k), c))

    greetings = 15 + 6 + 15

    src_copy = pltpu.make_async_copy(src_hbm, src, own_sem.at[5])
    inv_copy = pltpu.make_async_copy(inv_hbm, inv, own_sem.at[6])
    src_copy.start()
    inv_copy.start()

    def lag_copy(a):
        return pltpu.make_async_copy(lag.at[a], stage.at[a], lag_sem.at[a])

    for a in range(7):
        lag_copy(a).start()
    own_current = pltpu.make_async_copy(cur, cg.at[c], own_sem.at[0])
    own_current.start()

    def box(dr, dc):
        rows = {-1: (3, 15, 3), 1: (12, 0, 3), 0: (3, 3, 12)}[dr]
        cols = {-1: (8, 40, 8), 1: (32, 0, 8), 0: (8, 8, 32)}[dc]
        return rows, cols

    def halo_copy(s, d):
        dr, dc = DIRS[d]
        (rs, rd, rn), (cs, cd, cn) = box(dr, dc)
        return pltpu.make_async_remote_copy(
            src_ref=ext.at[s, pl.ds(rs, rn), pl.ds(cs, cn), :],
            dst_ref=ext.at[s, pl.ds(rd, rn), pl.ds(cd, cn), :],
            send_sem=send_sem.at[s, d],
            recv_sem=recv_sem.at[s, d],
            device_id=(wrap(r + dr), wrap(c + dc)),
            device_id_type=MESH,
        )

    side, place, core = c // 8, lax.rem(c // 2, 4), lax.rem(c, 2)
    partner = c + 1 - 2 * core
    across = lax.rem(c + 8, n)

    def ring(dx):
        return side * 8 + lax.rem(place + dx, 4) * 2 + core

    def ring_across(dx):
        return lax.rem(ring(dx) + 8, n)

    def current_copy(slot, col, sem):
        return pltpu.make_async_remote_copy(
            src_ref=cg.at[slot], dst_ref=cg.at[slot],
            send_sem=sem, recv_sem=cg_recv.at[slot],
            device_id=(r, col), device_id_type=MESH,
        )

    def own_sends():
        return [current_copy(c, ring(dx), cg_send.at[dx]) for dx in (1, 3, 2)] + [
            current_copy(c, across, cg_send.at[0]),
            current_copy(c, partner, cg_send.at[4]),
        ]

    def relays():
        return [current_copy(across, ring(dx), cg_relay.at[dx]) for dx in (1, 3, 2)]

    def early_passes():
        slots = [ring(1), ring(3), ring(2), across]
        return [current_copy(x, partner, cg_pass.at[k]) for k, x in enumerate(slots)]

    def late_passes():
        slots = [ring_across(1), ring_across(3), ring_across(2)]
        return [current_copy(x, partner, cg_pass.at[4 + k]) for k, x in enumerate(slots)]

    inv_copy.wait()
    src_copy.wait()
    b0h, b0l = split(inv[0])
    b1h, b1l = split(inv[1])
    put_embedded(vhi, 0, b0h, b1h)
    put_embedded(vlo, 0, b0l, b1l)

    def apply_inverse(x):
        xh, xl = split(x)
        return dot(xh, vhi[...]) + dot(xl, vhi[...]) + dot(xh, vlo[...])

    def source():
        re, im = field(src, slice(None), 0, 16)
        return jnp.concatenate([re.reshape(192, 128), im.reshape(192, 128)], axis=1)

    def publish(ref, at_, x):
        rows, start = at_
        ref[rows, pl.ds(start, 16, stride=2), :] = x[:, :128].reshape(12, 16, 128)
        ref[rows, pl.ds(start + 1, 16, stride=2), :] = x[:, 128:].reshape(12, 16, 128)

    adj[...] = apply_inverse(source())
    publish(ext.at[0], (slice(3, 15), 8), adj[...])
    own_current.wait()
    pl.semaphore_wait(barrier, greetings)

    def middle_first(t):
        return jnp.where(t == 0, 3, jnp.where(t < 4, t - 1, t))

    def sweep(s, carry):
        for d in range(len(DIRS)):
            halo_copy(s, d).start()
        @pl.when(s == 0)
        def _():
            for copy in own_sends():
                copy.start()

            def prepare(a, carry):
                lag_copy(a).wait()

                def one(b, carry):
                    h0, l0 = split(stage[a, b, 0])
                    h1, l1 = split(stage[a, b, 1])
                    base = pl.multiple_of(b * 256, 256)
                    put_embedded(whi.at[a], base, h0, h1)
                    put_embedded(wlo.at[a], base, l0, l1)
                    return carry

                return lax.fori_loop(0, 7, one, carry)

            lax.fori_loop(0, 7, prepare, 0)

        @pl.when(s > 0)
        def _():
            for copy in early_passes():
                copy.wait_recv()
                copy.start()
            for copy in relays():
                copy.start()

        def close_sides(rows, count):
            @pl.when(c == 0)
            def _():
                ext[s, rows, 0:8, :] = jnp.zeros((count, 8, 128), F32)

            @pl.when(c == n - 1)
            def _():
                ext[s, rows, 40:48, :] = jnp.zeros((count, 8, 128), F32)

        def build(rows):
            for b in range(7):
                for h in range(2):
                    hi, lo = split(ext[s, rows, pl.ds(2 * (b + 1) + h, 16, stride=2), :])
                    lanes = slice(b * 256 + h * 128, b * 256 + h * 128 + 128)
                    near_hi[rows, :, lanes] = hi
                    near_lo[rows, :, lanes] = lo

        for d in SIDES:
            halo_copy(s, d).wait_recv()
        close_sides(slice(3, 15), 12)
        build(slice(3, 15))
        total[...] = jnp.zeros_like(total)

        def lag_row(t, carry):
            a = middle_first(t)

            @pl.when(t == 1)
            def _():
                for d in REST:
                    halo_copy(s, d).wait_recv()

                @pl.when(r == 0)
                def _():
                    ext[s, 0:3] = jnp.zeros((3, 48, 128), F32)

                @pl.when(r == n - 1)
                def _():
                    ext[s, 15:18] = jnp.zeros((3, 48, 128), F32)

                close_sides(slice(0, 3), 3)
                close_sides(slice(15, 18), 3)
                build(slice(0, 3))
                build(slice(15, 18))

            hi = near_hi[pl.ds(a, 12)].reshape(192, 1792)
            lo = near_lo[pl.ds(a, 12)].reshape(192, 1792)
            total[...] += dot(hi, whi[a]) + dot(lo, whi[a]) + dot(hi, wlo[a])
            return carry

        lax.fori_loop(0, 7, lag_row, 0)
        adj[...] += apply_inverse(source() - adj[...] - total[...])
        @pl.when(s + 1 < SWEEPS)
        def _():
            publish(ext.at[lax.rem(s + 1, SWEEPS)], (slice(3, 15), 8), adj[...])

        return carry

    lax.fori_loop(0, SWEEPS, sweep, 0)

    for h in range(2):
        part = adj[:, h * 128:h * 128 + 128]
        part = jnp.concatenate([part, jnp.zeros((64, 128), F32)], axis=0)
        at[h] = part.T.reshape(16, 8, 256)

    def slice_copy(k, slot):
        return pltpu.make_async_remote_copy(
            src_ref=at.at[:, wrap(c + k)], dst_ref=ra.at[slot],
            send_sem=ra_send.at[k], recv_sem=ra_recv.at[k],
            device_id=(r, wrap(c + k)), device_id_type=MESH,
        )

    each(1, lambda k: slice_copy(k, c).start())
    own_slice = pltpu.make_async_copy(at.at[:, c], ra.at[c], own_sem.at[1])
    own_slice.start()
    publish(out_tile, (slice(None), 0), adj[...])
    out_copy = pltpu.make_async_copy(out_tile, out, out_sem.at[14])
    out_copy.start()

    for copy in late_passes():
        copy.wait_recv()
        copy.start()

    def convert(t):
        base = pl.multiple_of(t * 16, 16)
        for h in range(2):
            hi, lo = split(cg[t, :, pl.ds(h, 16, stride=2), :])
            chi[:, pl.ds(base, 16), h * 128:h * 128 + 128] = hi
            clo[:, pl.ds(base, 16), h * 128:h * 128 + 128] = lo

    for dx in range(4):
        other = ring(dx) + 1 - 2 * core
        current_copy(other, partner, cg_send.at[4]).wait_recv()
        current_copy(lax.rem(other + 8, n), partner, cg_send.at[4]).wait_recv()
    lax.fori_loop(0, n, lambda t, carry: (convert(t), carry)[1], 0)

    own_slice.wait()
    each(1, lambda k: slice_copy(k, wrap(c - k)).wait_recv())

    lane = lax.broadcasted_iota(jnp.int32, (16, 128), 1) // 16
    for i in range(12):
        block = slice((i // 8) * 128, (i // 8) * 128 + 128)
        for half in range(2):
            row = jnp.zeros((16, 128), F32)
            for t in range(8):
                x = ra[half * 8 + t, :, :, block].reshape(16, 128)
                shift = ((t - i % 8) * 16) % 128
                if shift:
                    x = pltpu.roll(x, shift, 1)
                row = jnp.where(lane == t, x, row)
            strip[3 + i, :, half * 128:half * 128 + 128] = row

    def edge_copy(d):
        src_, dst, to = ((3, 15, wrap(r - 1)), (12, 0, wrap(r + 1)))[d]
        return pltpu.make_async_remote_copy(
            src_ref=strip.at[pl.ds(src_, 3)], dst_ref=strip.at[pl.ds(dst, 3)],
            send_sem=halo_send.at[d], recv_sem=halo_recv.at[d],
            device_id=(to, c), device_id_type=MESH,
        )

    for d in range(2):
        edge_copy(d).start()

    column = lax.broadcasted_iota(jnp.int32, (16, 256), 1)

    def spread(e, carry):
        x = strip[e]
        for b in range(7):
            y = x if b == 3 else pltpu.roll(x, (3 - b) % 256, 1)
            if b < 3:
                y = jnp.where(column >= 3 - b, y, 0.0)
            if b > 3:
                y = jnp.where(column < 256 - (b - 3), y, 0.0)
            hi, lo = split(y)
            a7h[e, b * 16:b * 16 + 16, :] = hi
            a7l[e, b * 16:b * 16 + 16, :] = lo
        return carry

    lax.fori_loop(3, 15, spread, 0)

    def reduce_copy(p, slot):
        return pltpu.make_async_remote_copy(
            src_ref=terms.at[p], dst_ref=gathered.at[slot],
            send_sem=red_send.at[p], recv_sem=red_recv.at[slot],
            device_id=(p, c), device_id_type=MESH,
        )

    def keep_copy():
        return pltpu.make_async_copy(terms.at[r], gathered.at[r], own_sem.at[2])

    def correlate(t, carry):
        other = lax.rem(r // 2 + jnp.where(core == 0, t, 6 - t), 6)
        a = jnp.where(t == 0, 3, other + jnp.where(other >= 3, 1, 0))

        @pl.when(t == 1)
        def _():
            for d in range(2):
                edge_copy(d).wait_recv()

            @pl.when(r == 0)
            def _():
                strip[0:3] = jnp.zeros((3, 16, 256), F32)

            @pl.when(r == n - 1)
            def _():
                strip[15:18] = jnp.zeros((3, 16, 256), F32)

            lax.fori_loop(0, 3, spread, 0)
            lax.fori_loop(15, 18, spread, 0)

        high = jnp.concatenate([a7h[a + i] for i in range(12)], axis=1)
        low = jnp.concatenate([a7l[a + i] for i in range(12)], axis=1)
        both = dot(jnp.concatenate([high, low], axis=0), chi[...].reshape(3072, 256))
        rest = dot(high, clo[...].reshape(3072, 256))
        x = (both[0:112] + both[112:224] + rest).reshape(7, 2, 8, 256)
        real = (x[:, 0, :, 0:128] + x[:, 1, :, 128:256]) * factor
        imag = (x[:, 1, :, 0:128] - x[:, 0, :, 128:256]) * factor
        for b in range(7):
            for h, part in ((0, real), (1, imag)):
                tile = b * 2 + h
                terms[a * 2 + tile // 7, tile % 7] = part[b]
        for e in range(2):
            p = a * 2 + e

            @pl.when(p != r)
            def _():
                reduce_copy(p, r).start()

            @pl.when(p == r)
            def _():
                keep_copy().start()

        return carry

    lax.fori_loop(0, 7, correlate, 0)

    @pl.when(r < 14)
    def _():
        def collect(k, carry):
            @pl.when(k == r)
            def _():
                keep_copy().wait()

            @pl.when(k != r)
            def _():
                reduce_copy(r, k).wait_recv()

            return carry

        lax.fori_loop(0, n, collect, 0)
        x = gathered[0]
        for k in range(1, n):
            x = x + gathered[k]
        piece[...] = x

    def swap_copy():
        return pltpu.make_async_remote_copy(
            src_ref=piece, dst_ref=swapped, send_sem=swap_send, recv_sem=swap_recv,
            device_id=(c, r), device_id_type=MESH,
        )

    @pl.when(jnp.logical_and(r != c, r < 14))
    def _():
        swap_copy().start()

    @pl.when(jnp.logical_and(r != c, c < 14))
    def _():
        swap_copy().wait_recv()

    @pl.when(jnp.logical_and(r == c, r < 14))
    def _():
        own = pltpu.make_async_copy(piece, swapped, own_sem.at[3])
        own.start()
        own.wait()

    @pl.when(jnp.logical_and(r != c, r < 14))
    def _():
        swap_copy().wait_send()

    def result_copy(k, slot):
        return pltpu.make_async_remote_copy(
            src_ref=swapped, dst_ref=result.at[slot],
            send_sem=res_send.at[k], recv_sem=res_recv.at[slot],
            device_id=(r, wrap(c + k)), device_id_type=MESH,
        )

    own_result = pltpu.make_async_copy(swapped, result.at[c], own_sem.at[4])

    @pl.when(c < 14)
    def _():
        each(1, lambda k: result_copy(k, c).start())
        own_result.start()

    def drain_reduce(p, carry):
        @pl.when(p != r)
        def _():
            reduce_copy(p, r).wait_send()

        return carry

    lax.fori_loop(0, 14, drain_reduce, 0)
    each(1, lambda k: slice_copy(k, c).wait_send())
    for copy in own_sends() + relays() + early_passes() + late_passes():
        copy.wait_send()
    for d in range(2):
        edge_copy(d).wait_send()
    for s in range(SWEEPS):
        for d in range(len(DIRS)):
            halo_copy(s, d).wait_send()

    def grad_copy(p):
        return pltpu.make_async_copy(result.at[p], grad.at[pl.ds(p * 7, 7)], out_sem.at[p])

    def finish(p, carry):
        @pl.when(p == c)
        def _():
            own_result.wait()

        @pl.when(p != c)
        def _():
            result_copy(1, p).wait_recv()

        grad_copy(p).start()
        return carry

    lax.fori_loop(0, 14, finish, 0)
    out_copy.wait()
    lax.fori_loop(0, 14, lambda p, carry: (grad_copy(p).wait(), carry)[1], 0)

    @pl.when(c < 14)
    def _():
        each(1, lambda k: result_copy(k, c).wait_send())


def hand_out(adj, grad, adj_out, grad_out, adj_buf, grad_buf, sem):
    into = [
        pltpu.make_async_copy(adj, adj_buf, sem.at[0]),
        pltpu.make_async_copy(grad, grad_buf, sem.at[1]),
    ]
    back = [
        pltpu.make_async_copy(adj_buf, adj_out, sem.at[2]),
        pltpu.make_async_copy(grad_buf, grad_out, sem.at[3]),
    ]
    for copy in into:
        copy.start()
    for first, second in zip(into, back):
        first.wait()
        second.start()
    for copy in back:
        copy.wait()


def on_device(adjoint_source, saved_currents, lag_blocks, element_inverse):
    hbm = pl.BlockSpec(memory_space=pl.ANY)
    dma = pltpu.SemaphoreType.DMA
    elements = 12 * lax.axis_size("row") * 16 * lax.axis_size("col")
    adjoint, lag_grad = pl.pallas_call(
        functools.partial(kernel, -1.0 / math.sqrt(elements)),
        out_shape=(
            jax.ShapeDtypeStruct((12, 32, 128), F32),
            jax.ShapeDtypeStruct((98, 8, 128), F32),
        ),
        in_specs=[pl.BlockSpec(memory_space=pltpu.HBM)] * 4,
        out_specs=(pl.BlockSpec(memory_space=pltpu.HBM),) * 2,
        scratch_shapes=[
            pltpu.VMEM((12, 32, 128), F32),
            pltpu.VMEM((2, 128, 128), F32),
            pltpu.VMEM((12, 32, 128), F32),
            pltpu.VMEM((7, 7, 2, 128, 128), F32),
            pltpu.VMEM((7, 1792, 256), BF16),
            pltpu.VMEM((7, 1792, 256), BF16),
            pltpu.VMEM((256, 256), BF16),
            pltpu.VMEM((256, 256), BF16),
            pltpu.VMEM((SWEEPS, 18, 48, 128), F32),
            pltpu.VMEM((18, 16, 1792), BF16),
            pltpu.VMEM((18, 16, 1792), BF16),
            pltpu.VMEM((192, 256), F32),
            pltpu.VMEM((192, 256), F32),
            pltpu.VMEM((16, 12, 32, 128), F32),
            pltpu.VMEM((12, 256, 256), BF16),
            pltpu.VMEM((12, 256, 256), BF16),
            pltpu.VMEM((2, 16, 8, 256), F32),
            pltpu.VMEM((16, 2, 8, 256), F32),
            pltpu.VMEM((18, 16, 256), F32),
            pltpu.VMEM((18, 112, 256), BF16),
            pltpu.VMEM((18, 112, 256), BF16),
            pltpu.VMEM((14, 7, 8, 128), F32),
            pltpu.VMEM((16, 7, 8, 128), F32),
            pltpu.VMEM((7, 8, 128), F32),
            pltpu.VMEM((7, 8, 128), F32),
            pltpu.VMEM((16, 7, 8, 128), F32),
            dma((7,)), dma((SWEEPS, 8)), dma((SWEEPS, 8)),
            dma((5,)), dma((4,)), dma((7,)), dma((16,)),
            dma((16,)), dma((16,)), dma((2,)), dma((2,)),
            dma((16,)), dma((16,)), dma(()), dma(()), dma((16,)), dma((16,)), dma((7,)), dma((15,)),
        ],
        compiler_params=pltpu.CompilerParams(
            collective_id=0, has_side_effects=True, vmem_limit_bytes=62 * 1024 * 1024
        ),
        name="adjoint_gradient",
    )(
        adjoint_source.reshape(12, 32, 128),
        saved_currents.reshape(12, 32, 128),
        lag_blocks,
        element_inverse,
    )
    adjoint, lag_grad = pl.pallas_call(
        hand_out,
        out_shape=(
            jax.ShapeDtypeStruct((12, 32, 128), F32),
            jax.ShapeDtypeStruct((98, 8, 128), F32),
        ),
        in_specs=[hbm, hbm],
        out_specs=(hbm, hbm),
        scratch_shapes=[
            pltpu.VMEM((12, 32, 128), F32), pltpu.VMEM((98, 8, 128), F32), dma((4,)),
        ],
        compiler_params=pltpu.CompilerParams(vmem_limit_bytes=62 * 1024 * 1024),
        name="hand_out",
    )(adjoint, lag_grad)
    return (adjoint.reshape(12, 16, 2, 128), lag_grad.reshape(7, 7, 2, 8, 128))


def solution(mesh):
    return jax.shard_map(
        on_device,
        mesh=mesh,
        in_specs=(P("row", "col", None, None), P("row", "col", None, None), P(), P()),
        out_specs=(P("row", "col", None, None), P(None, None, None, "row", None)),
        check_vma=False,
    )
```
